128 devices in a mesh: comp: 32 (over z, y, core), lat: 4 (over x).
Axes of the slice: x: 4, y: 4, z: 4, core: 2. Of those that a mesh axis runs over, the one named last changes fastest.
Arguments:
- spectrum: float32 [32, 36, 384, 512], P('comp', None, 'lat'), may hold values from 0.1 to 3
- sea_mask: int32 [384, 512], P('lat'), may hold values from 0 to 1, as said below
- point_index: int32 [4, 32768], P('lat'), may hold values from 0 to 49151, as said below
- band_counts: int32 [4], P('lat'), may hold values from 16384 to 32768, as said below
- sub_counts: int32 [32], P('comp'), may hold values from 2 to 4, as said below
- mix_in: bfloat16 [1152, 1152], replicated, may hold values from -0.1875 to 0.1875
- mix_out: bfloat16 [1152, 1152], replicated, may hold values from -0.1875 to 0.1875
- growth: float32 [32, 36], replicated, may hold values from 0.05 to 1
- damping: float32 [32, 36], replicated, may hold values from 0.1 to 2
Outputs:
- new_spectrum: float32 [32, 36, 384, 512], P('comp', None, 'lat')
The draws below stay inside these ranges and needn't reach their ends.
Inputs may be any that keep to these rules, and one draw needn't show every extreme that they name: `sea_mask`: exactly band_counts[b] of the 49152 cells of band b are sea. `point_index`: row b lists the sea cells of band b in increasing order in its first band_counts[b] slots, zeros after them. `band_counts`: some band has exactly 32768 sea cells. `sub_counts`: some frequency has exactly 4 substeps.
All inputs are finite; a program needn't handle non-finite values.
Results may differ from the reference program's by a relative error of at most 0.0015.
Values may be sent and summed in bfloat16 or wider, within the bound.
A program may use at most 128 MiB of HBM per device.

```python
import math
import jax
import jax.numpy as jnp
from jax import lax

NDIR = 36
NFREQ = 32
ROWS = 96
LON = 512
NSUB = 4
K = 1152
BANDS = 4
NY = 384
PCAP = 32768


def sea_layout(key):
    base_key = jax.random.fold_in(key, 7)
    subkeys = jax.random.split(base_key, 4)
    counts = jax.random.randint(subkeys[0], (BANDS,), PCAP // 2, PCAP + 1)
    top_band = jax.random.randint(subkeys[1], (), 0, BANDS)
    counts = jnp.where(jnp.arange(BANDS) == top_band, PCAP, counts)
    coarse = jax.random.randint(subkeys[2], (BANDS, (ROWS + 7) // 8, (LON + 7) // 8), 0, 16)
    coarse = jnp.repeat(jnp.repeat(coarse, 8, axis=1), 8, axis=2)[:, :ROWS, :LON]
    fine_level = jax.random.randint(subkeys[3], (BANDS, ROWS, LON), 0, 64)
    cell_count = ROWS * LON
    cell_ids = jnp.arange(cell_count, dtype=jnp.int32)
    scores = ((coarse * 64 + fine_level) * cell_count).reshape(BANDS, cell_count) + cell_ids[None, :]
    cell_rank = jnp.argsort(jnp.argsort(scores, axis=1), axis=1)
    sea_cells = cell_rank < counts[:, None]
    order_key = jnp.where(sea_cells, cell_ids[None, :], cell_count + cell_ids[None, :])
    listed = jnp.argsort(order_key, axis=1)[:, :PCAP]
    listed = jnp.where(jnp.arange(PCAP)[None, :] < counts[:, None], listed, 0)
    return (sea_cells.astype(jnp.int32), listed.astype(jnp.int32), counts.astype(jnp.int32))


def draw_sea_mask(key, part):
    return sea_layout(key)[0].reshape(BANDS * ROWS, LON)


def draw_point_index(key, part):
    return sea_layout(key)[1]


def draw_band_counts(key, part):
    return sea_layout(key)[2]


def draw_sub_counts(key, part):
    base_key = jax.random.fold_in(key, 13)
    subkeys = jax.random.split(base_key, 2)
    steps_drawn = jax.random.randint(subkeys[0], (NFREQ,), 2, NSUB + 1)
    top_freq = jax.random.randint(subkeys[1], (), 0, NFREQ)
    return jnp.where(jnp.arange(NFREQ) == top_freq, NSUB, steps_drawn).astype(jnp.int32)


def levels(stream_key, shape, shards, least, high):
    gain = 1.0
    for axis_at, parts in shards:
        draws = jax.random.uniform(jax.random.fold_in(jax.random.fold_in(stream_key, 6), axis_at), (parts,), jnp.float32, least / len(shards), high / len(shards))
        gain = gain * jnp.repeat(jnp.exp(draws), shape[axis_at] // parts).reshape((-1,) + (1,) * (len(shape) - 1 - axis_at))
    return gain


def noise(rng, extent, deviation, bound, kind=jnp.bfloat16):
    array = jax.random.normal(rng, extent, jnp.float32) * deviation
    return jnp.minimum(jnp.maximum(array, -bound), bound).astype(kind)


def setup_inputs(seed: int = 0) -> dict:
    key_of = jax.random.split(jax.random.key(seed), 10)
    return {
        "spectrum": jnp.clip(jnp.exp(math.log(3.0) - 3.4011974 * jax.random.uniform(key_of[0], (NFREQ, NDIR, NY, LON), jnp.float32) ** levels(key_of[0], (NFREQ, NDIR, NY, LON), ((0, 32), (2, 4)), -0.2, 0.2)), 0.1, 3.0),
        "sea_mask": draw_sea_mask(jax.random.fold_in(key_of[9], 71), 0),
        "point_index": draw_point_index(jax.random.fold_in(key_of[9], 71), 0),
        "band_counts": draw_band_counts(jax.random.fold_in(key_of[9], 71), 0),
        "sub_counts": draw_sub_counts(jax.random.fold_in(key_of[9], 71), 0),
        "mix_in": noise(key_of[5], (K, K), K ** -0.5, 0.1875),
        "mix_out": noise(key_of[6], (K, K), K ** -0.5, 0.1875),
        "growth": jnp.clip(jnp.exp(jax.random.uniform(key_of[7], (NFREQ, NDIR), jnp.float32, math.log(0.05), math.log(1.0))), 0.05, 1.0),
        "damping": jnp.clip(jnp.exp(jax.random.uniform(key_of[8], (NFREQ, NDIR), jnp.float32, math.log(0.1), math.log(2.0))), 0.1, 2.0),
    }


def next_column(values_in):
    return jnp.concatenate([values_in[..., 1:], jnp.zeros_like(values_in[..., :1])], axis=-1)


def prev_column(values_in):
    return jnp.concatenate([jnp.zeros_like(values_in[..., :1]), values_in[..., :-1]], axis=-1)


def openings(mask_rows):
    inner_mask = mask_rows[1:-1]
    open_lon = inner_mask * next_column(inner_mask)
    open_lat = mask_rows[:-1] * mask_rows[1:]
    return open_lon, open_lat


def advance(padded, open_lon, open_lat, courant_x, courant_y):
    inner_rows = padded[..., 1:-1, :]
    flux_lon = (jnp.maximum(courant_x, 0.0) * inner_rows + jnp.minimum(courant_x, 0.0) * next_column(inner_rows)) * open_lon
    flux_lat = (jnp.maximum(courant_y, 0.0) * padded[..., :-1, :] + jnp.minimum(courant_y, 0.0) * padded[..., 1:, :]) * open_lat
    return inner_rows - flux_lon + prev_column(flux_lon) - flux_lat[..., 1:, :] + flux_lat[..., :-1, :]


def courant(freq_index, sub_steps, substep, dir_count):
    group_speed = 1.4 * jnp.power(0.93, freq_index.astype(jnp.float32))
    active = (sub_steps > substep).astype(jnp.float32)
    per_step = group_speed * active / sub_steps.astype(jnp.float32)
    angles = (jnp.arange(dir_count, dtype=jnp.float32) + 0.5) * (2.0 * jnp.pi / dir_count)
    return per_step[..., None] * jnp.cos(angles), per_step[..., None] * jnp.sin(angles)


def freq_weights(freq_count, dir_count):
    raw_weight = jnp.power(1.1, jnp.arange(freq_count, dtype=jnp.float32))
    raw_weight = raw_weight / (dir_count * jnp.sum(raw_weight))
    return jnp.repeat(raw_weight, dir_count)


def source_increment(points, growth_col, damping_col, mix_in, mix_out, freq_weight):
    energy = points.astype(jnp.float32)
    hidden = jnp.dot(mix_in, points, preferred_element_type=jnp.float32)
    square = (hidden * hidden).astype(jnp.bfloat16)
    transfer = jnp.dot(mix_out, square, preferred_element_type=jnp.float32)
    mean_energy = jnp.sum(freq_weight[:, None] * energy, axis=0)
    increment = 0.5 * (growth_col * energy + 0.25 * transfer - damping_col * energy * (mean_energy / (1.0 + mean_energy)))
    return increment.astype(jnp.bfloat16)


def reference(spectrum, sea_mask, point_index, band_counts, sub_counts, mix_in, mix_out, growth, damping):
    mask_float = sea_mask.astype(jnp.float32)
    mask_ext = jnp.pad(mask_float, ((1, 1), (0, 0)))
    open_lon, open_lat = openings(mask_ext)

    def propagate_freq(packed):
        wave_field, freq_index, sub_steps = packed
        wave_field = wave_field * mask_float
        for substep in range(NSUB):
            courant_x, courant_y = courant(freq_index, sub_steps, substep, NDIR)
            padded = jnp.pad(wave_field, ((0, 0), (1, 1), (0, 0)))
            wave_field = advance(padded, open_lon, open_lat, courant_x[:, None, None], courant_y[:, None, None])
        return wave_field

    propagated = lax.map(propagate_freq, (spectrum, jnp.arange(NFREQ, dtype=jnp.int32), sub_counts))
    freq_weight = freq_weights(NFREQ, NDIR)
    growth_col = growth.reshape(K, 1)
    damping_col = damping.reshape(K, 1)
    band_fields = []
    for band_index in range(BANDS):
        flat_field = propagated[:, :, band_index * ROWS:(band_index + 1) * ROWS, :].reshape(K, ROWS * LON)
        listed = point_index[band_index]
        points = jnp.take(flat_field.astype(jnp.bfloat16), listed, axis=1)
        increment = source_increment(points, growth_col, damping_col, mix_in, mix_out, freq_weight)
        in_range = (jnp.arange(PCAP) < band_counts[band_index]).astype(jnp.float32)
        flat_field = flat_field.at[:, listed].add(increment.astype(jnp.float32) * in_range[None, :])
        band_fields.append(flat_field.reshape(NFREQ, NDIR, ROWS, LON))
    return jnp.concatenate(band_fields, axis=2)
```

```python
import functools
import math

import jax
import jax.numpy as jnp
import numpy as np
from jax import lax
from jax.experimental import pallas as pl
from jax.experimental.pallas import tpu as pltpu
from jax.sharding import PartitionSpec as P

MESH = pl.DeviceIdType.MESH
F32, BF16 = jnp.float32, jnp.bfloat16
NSUB = 4
NDIR, NFREQ, ROWS, LON = 36, 32, 96, 512
K = NDIR * NFREQ
GROUPS = 32
CHUNKS = ROWS // GROUPS
HALO = 4
EDGE = 8
SIDE = ROWS + EDGE
MAIN = 32
MSG = 4 * MAIN + 16
HID = 1184
TILE1 = HID // 2
TILE2 = 512
BLOCK = 8

LATIN = [((i + dy) % 4, dy) for i in range(4) for dy in (1, 3, 2, 0) if ((i + dy) % 4, dy) != (0, 0)]
ORDER = [(dz, dy, dc) for dz, dy in LATIN for dc in (0, 1)] + [(0, 0, 1)]


def direction(quadrant, place):
    return 9 * quadrant + place


def angle_tables():
    main = [direction(q, t) for q in range(4) for t in range(8)]
    left_plus = [direction(i, 8) for _ in range(4) for i in range(2)]
    left_minus = [direction(2 + i, 8) for _ in range(4) for i in range(2)]
    angles = (np.array(main + left_plus + left_minus, np.float32) + np.float32(0.5)) * np.float32(2.0 * np.pi / NDIR)
    table = np.stack([np.abs(np.cos(angles)), np.abs(np.sin(angles))]).astype(np.float32)
    return np.ascontiguousarray(np.broadcast_to(table[:, :, None], (2, 48, 128)))


def natural(c):
    k = c & 31
    main = 36 * (c >> 5) + 9 * (k >> 3) + (k & 7)
    r = c - 1024
    left = 36 * ((r & 63) >> 1) + 9 * (2 * (r & 1) + (r >> 6)) + 8
    return jnp.where(c < 1024, main, left)


def kernel(
    spec, mask, scal, table, w_in, w_out, mean_w, gain, damp,
    out,
    fp, fm, lp, lm, msk, mh, ox, oxm, oy, oym, oxl, oyl, ml,
    pb, rm, ib, ri, win, wout, perm, wi, wo, sq, hq, lf, rl, tl,
    in_sem, halo_send, halo_recv, mask_send, mask_recv, lmask_sem, w_sem, own_sem,
    send_sem, recv_sem, back_send, back_recv, out_sem,
):
    me, lat = lax.axis_index("comp"), lax.axis_index("lat")
    z, y, core = lax.div(me, 8), lax.rem(lax.div(me, 2), 4), lax.rem(me, 2)
    partners = [
        (lax.rem(z + dz, 4) * 4 + lax.rem(y + dy, 4)) * 2 + lax.rem(core + dc, 2) for dz, dy, dc in ORDER
    ]

    for quadrant in range(4):
        dst, base, sem = (fp, EDGE, 0) if quadrant < 2 else (fm, 0, 1)
        for t in range(8):
            slot = 8 * (quadrant % 2) + t
            pltpu.make_async_copy(
                spec.at[0, direction(quadrant, t)], dst.at[pl.ds(base, ROWS), slot, :], in_sem.at[sem]
            ).start()
        dst, sem = (lp, 2) if quadrant < 2 else (lm, 3)
        for ct in range(4):
            pltpu.make_async_copy(
                spec.at[0, direction(quadrant, 8), :, pl.ds(128 * ct, 128)],
                dst.at[pl.ds(base, ROWS), 2 * ct + quadrant % 2, :],
                in_sem.at[sem],
            ).start()
    w_copies = [
        pltpu.make_async_copy(w_in, win, w_sem.at[0]),
        pltpu.make_async_copy(w_out, wout, w_sem.at[1]),
    ]
    for copy in w_copies:
        copy.start()

    barrier = pltpu.get_barrier_semaphore()
    for partner in partners:
        pl.semaphore_signal(barrier, inc=1, device_id=(partner, lat), device_id_type=MESH)
    inner_low, inner_high = lat > 0, lat < 3

    @pl.when(inner_low)
    def _():
        pl.semaphore_signal(barrier, inc=1, device_id=(me, lat - 1), device_id_type=MESH)

    @pl.when(inner_high)
    def _():
        pl.semaphore_signal(barrier, inc=1, device_id=(me, lat + 1), device_id_type=MESH)

    neighbours = jnp.where(inner_low, 1, 0) + jnp.where(inner_high, 1, 0)
    pl.semaphore_wait(barrier, len(ORDER) + neighbours)

    def mask_copy(up):
        return pltpu.make_async_remote_copy(
            mask.at[pl.ds(88, 8)] if up else mask.at[pl.ds(0, 8)],
            mh.at[0 if up else 1],
            mask_send.at[0 if up else 1],
            mask_recv.at[0 if up else 1],
            device_id=(me, lat + 1 if up else lat - 1),
            device_id_type=MESH,
        )

    def halo_copies(up):
        side = 0 if up else 1
        target = (me, lat + 1 if up else lat - 1)
        field, left = (fp, lp) if up else (fm, lm)
        src, dst = (SIDE - HALO, EDGE - HALO) if up else (0, ROWS)
        return [
            pltpu.make_async_remote_copy(
                ref.at[pl.ds(src, HALO)], ref.at[pl.ds(dst, HALO)], halo_send.at[side, i], halo_recv.at[side, i],
                device_id=target, device_id_type=MESH,
            )
            for i, ref in enumerate((field, left))
        ]

    @pl.when(inner_high)
    def _():
        mask_copy(True).start()

    @pl.when(inner_low)
    def _():
        mask_copy(False).start()

    for sem, ref, base in ((0, fp, EDGE), (2, lp, EDGE)):
        pltpu.make_async_copy(ref.at[pl.ds(base, ROWS)], ref.at[pl.ds(base, ROWS)], in_sem.at[sem]).wait()

    @pl.when(inner_high)
    def _():
        for copy in halo_copies(True):
            copy.start()

    for sem, ref, base in ((1, fm, 0), (3, lm, 0)):
        pltpu.make_async_copy(ref.at[pl.ds(base, ROWS)], ref.at[pl.ds(base, ROWS)], in_sem.at[sem]).wait()

    @pl.when(inner_low)
    def _():
        for copy in halo_copies(False):
            copy.start()

    @pl.when(inner_low)
    def _():
        mask_copy(True).wait_recv()

    @pl.when(jnp.logical_not(inner_low))
    def _():
        mh[0] = jnp.zeros((8, LON), jnp.int32)
        fp[pl.ds(HALO, HALO)] = jnp.zeros((HALO, 16, LON), F32)
        lp[pl.ds(HALO, HALO)] = jnp.zeros((HALO, 8, 128), F32)

    @pl.when(inner_high)
    def _():
        mask_copy(False).wait_recv()

    @pl.when(jnp.logical_not(inner_high))
    def _():
        mh[1] = jnp.zeros((8, LON), jnp.int32)
        fm[pl.ds(ROWS, HALO)] = jnp.zeros((HALO, 16, LON), F32)
        lm[pl.ds(ROWS, HALO)] = jnp.zeros((HALO, 8, 128), F32)

    for ref, at in ((fp, 0), (fm, SIDE - HALO)):
        ref[pl.ds(at, HALO)] = jnp.zeros((HALO, 16, LON), F32)
    for ref, at in ((lp, 0), (lm, SIDE - HALO)):
        ref[pl.ds(at, HALO)] = jnp.zeros((HALO, 8, 128), F32)
    whole = jnp.concatenate([mh[0], mask[...], mh[1]], axis=0).astype(F32)
    column = lax.broadcasted_iota(jnp.int32, (112, LON), 1)
    for ref, value in (
        (msk, whole),
        (ox, jnp.where(column < LON - 1, whole * pltpu.roll(whole, LON - 1, 1), 0.0)),
        (oxm, jnp.where(column > 0, whole * pltpu.roll(whole, 1, 1), 0.0)),
        (oy, whole * pltpu.roll(whole, 111, 0)),
        (oym, whole * pltpu.roll(whole, 1, 0)),
    ):
        ref[...] = value.reshape(14, 8, LON)
    for ct in range(4):
        cols = pl.ds(128 * ct, 128)
        for i in range(2):
            place = 2 * ct + i
            for src, dst in (
                (oxm if i else ox, oxl.at[0]), (ox if i else oxm, oxl.at[1]),
                (oy, oyl.at[0]), (oym, oyl.at[1]), (msk, ml),
            ):
                pltpu.make_async_copy(src.at[:, :, cols], dst.at[:, :, place, :], lmask_sem.at[0]).start()
    for ref in (oxl, oyl, ml):
        pltpu.make_async_copy(ref, ref, lmask_sem.at[0]).wait()

    @pl.when(inner_low)
    def _():
        for copy in halo_copies(True):
            copy.wait_recv()

    @pl.when(inner_high)
    def _():
        for copy in halo_copies(False):
            copy.wait_recv()

    @pl.when(inner_high)
    def _():
        mask_copy(True).wait_send()
        for copy in halo_copies(True):
            copy.wait_send()

    @pl.when(inner_low)
    def _():
        mask_copy(False).wait_send()
        for copy in halo_copies(False):
            copy.wait_send()

    lane = lax.broadcasted_iota(jnp.int32, (8, 128), 1)
    odd = lax.rem(lax.broadcasted_iota(jnp.int32, (8, 128), 0), 2) == 1

    def wide(v):
        return jnp.concatenate([v] * 4, axis=1)

    def propagate(field, left, side, substep):
        a = scal[substep]
        coef = [
            (wide(a * table[0, pl.ds(16 * side + 8 * g, 8), :]), wide(a * table[1, pl.ds(16 * side + 8 * g, 8), :]))
            for g in range(2)
        ]
        coef_l = (a * table[0, pl.ds(32 + 8 * side, 8), :], a * table[1, pl.ds(32 + 8 * side, 8), :])
        open_y = oy if side == 0 else oym

        def block(b, carry):
            flows = list(carry)
            for step in range(BLOCK):
                j = step if side == 0 else BLOCK - 1 - step
                block_at = b if side == 0 else SIDE // BLOCK - 1 - b
                i = block_at * BLOCK + j
                e = (block_at + side, j)
                row = (block_at + side, slice(j, j + 1), slice(None))
                oy_row = open_y[row]
                for g in range(2):
                    right = g == side
                    x = field[i, pl.ds(8 * g, 8), :]
                    if substep == 0:
                        x = x * msk[row]
                    o = x * coef[g][0] * (ox if right else oxm)[row]
                    p = x * coef[g][1] * oy_row
                    inflow = pltpu.roll(o, 1 if right else LON - 1, 1)
                    field[i, pl.ds(8 * g, 8), :] = x - o + inflow - p + flows[g]
                    flows[g] = p
                x = left[i]
                if substep == 0:
                    x = x * ml[e]
                o = x * coef_l[0] * oxl[(side, *e)]
                p = x * coef_l[1] * oyl[(side, *e)]
                up = pltpu.roll(o, 1, 1)
                up = jnp.where(lane == 0, pltpu.roll(up, 2, 0), up)
                down = pltpu.roll(o, 127, 1)
                down = jnp.where(lane == 127, pltpu.roll(down, 6, 0), down)
                inflow = jnp.where(odd, down, up) if side == 0 else jnp.where(odd, up, down)
                left[i] = x - o + inflow - p + flows[2]
                flows[2] = p
            return tuple(flows)

        zero = jnp.zeros((8, LON), F32)
        lax.fori_loop(0, SIDE // BLOCK, block, (zero, zero, jnp.zeros((8, 128), F32)))

    for substep in range(NSUB):
        for side in range(2):
            propagate((fp, fm)[side], (lp, lm)[side], side, substep)

    def points(q):
        def row(j, _):
            r = q * GROUPS + j
            for ct in range(4):
                cols = pl.ds(128 * ct, 128)
                pb[r, pl.ds(MAIN * ct, 16), :] = fp[r + EDGE, :, cols].astype(BF16)
                pb[r, pl.ds(MAIN * ct + 16, 16), :] = fm[r, :, cols].astype(BF16)
            pb[r, pl.ds(4 * MAIN, 16), :] = jnp.concatenate([lp[r + EDGE], lm[r]], axis=0).astype(BF16)
            return 0

        lax.fori_loop(0, GROUPS, row, 0)

    def send_copy(q, partner):
        return pltpu.make_async_remote_copy(
            pb.at[q * GROUPS + partner], rm.at[q, me], send_sem.at[q], recv_sem.at[q],
            device_id=(partner, lat), device_id_type=MESH,
        )

    def back_copy(q, partner):
        return pltpu.make_async_remote_copy(
            ib.at[q, partner], ri.at[q * GROUPS + me], back_send.at[q], back_recv.at[q],
            device_id=(partner, lat), device_id_type=MESH,
        )

    for q in range(CHUNKS):
        points(q)
        for partner in partners:
            send_copy(q, partner).start()
        pltpu.make_async_copy(pb.at[q * GROUPS + me], rm.at[q, me], recv_sem.at[q]).start()

    for copy in w_copies:
        copy.wait()

    def select_columns(i, _):
        rows = pl.ds(pl.multiple_of(i * 384, 384), 384)
        wi[rows, :] = jnp.dot(win[rows, :], perm[...], preferred_element_type=F32).astype(BF16)
        return 0

    def select_rows(i, _):
        rows = pl.ds(pl.multiple_of(i * 384, 384), 384)
        wo[rows, pl.ds(0, K)] = jnp.dot(perm[rows, :], wout[...], preferred_element_type=F32).astype(BF16)
        return 0

    def build(across):
        def tile(i, _):
            start = pl.multiple_of(i * 128, 128)
            rows = start + lax.broadcasted_iota(jnp.int32, (128, K), 0)
            cols = lax.broadcasted_iota(jnp.int32, (128, K), 1)
            hit = natural(cols) == rows if across else natural(rows) == cols
            perm[pl.ds(start, 128), :] = jnp.where(hit, 1.0, 0.0).astype(BF16)
            return 0

        lax.fori_loop(0, K // 128, tile, 0)

    build(True)
    lax.fori_loop(0, 3, select_columns, 0)
    wi[pl.ds(K, HID - K), :] = mean_w[...]
    build(False)
    lax.fori_loop(0, 3, select_rows, 0)
    wo[:, pl.ds(K, HID - K)] = jnp.zeros((K, HID - K), BF16)

    def sources(q):
        lf[...] = rm[q, :, pl.ds(4 * MAIN, 16), :].reshape(16 * GROUPS, 128).astype(F32)
        for ct in range(4):
            for i in range(2):
                rl[pl.ds(64 * i, 64), pl.ds(128 * ct, 128)] = lf[pl.ds(2 * ct + i, 64, stride=8), :].astype(BF16)

        def right_side():
            main = [rm[q, :, pl.ds(MAIN * ct, MAIN), :].reshape(MAIN * GROUPS, 128) for ct in range(4)]
            return jnp.concatenate([jnp.concatenate(main, axis=1), rl[...]], axis=0)

        for part in range(2):
            hidden = jnp.dot(wi[pl.ds(TILE1 * part, TILE1), :], right_side(), preferred_element_type=F32)
            sq[pl.ds(TILE1 * part, TILE1), :] = (hidden * hidden).astype(BF16)
            if part == 1:
                energy = hidden[K - TILE1 : K - TILE1 + 1] + hidden[K - TILE1 + 1 : K - TILE1 + 2]
                hq[...] = jnp.broadcast_to(energy / (1.0 + energy), (8, LON))
        square = sq[...]

        def rows_of(i, _):
            base = pl.multiple_of(i * TILE2, TILE2)
            dests = TILE2 // MAIN
            transfer = jnp.dot(wo[pl.ds(base, TILE2), :], square, preferred_element_type=F32)
            for ct in range(4):
                where = (q, pl.ds(i * dests, dests), pl.ds(MAIN * ct, MAIN), slice(None))
                energy = rm[where].astype(F32).reshape(TILE2, 128)
                rate = gain[pl.ds(base, TILE2), :] - damp[pl.ds(base, TILE2), :] * hq[0:1, 128 * ct : 128 * ct + 128]
                result = energy * rate + 0.125 * transfer[:, 128 * ct : 128 * ct + 128]
                ib[where] = result.astype(BF16).reshape(dests, MAIN, 128)
            return 0

        lax.fori_loop(0, MAIN * GROUPS // TILE2, rows_of, 0)
        transfer = jnp.dot(wo[pl.ds(1024, 128), :], square, preferred_element_type=F32)
        for ct in range(4):
            cols = slice(128 * ct, 128 * ct + 128)
            rate = gain[pl.ds(1024, 128), :] - damp[pl.ds(1024, 128), :] * hq[0:1, cols]
            result = rl[:, cols].astype(F32) * rate + 0.125 * transfer[:, cols]
            for i in range(2):
                tl[pl.ds(2 * ct + i, 64, stride=8), :] = result[64 * i : 64 * i + 64]
        ib[q, :, pl.ds(4 * MAIN, 16), :] = tl[...].astype(BF16).reshape(GROUPS, 16, 128)

    def chunk(q, _):
        pltpu.make_async_copy(rm.at[q], rm.at[q], recv_sem.at[q]).wait()
        sources(q)
        for partner in partners:
            back_copy(q, partner).start()
        pltpu.make_async_copy(ib.at[q, me], ri.at[q * GROUPS + me], back_recv.at[q]).start()
        return 0

    lax.fori_loop(0, CHUNKS, chunk, 0)

    def store_copies(q):
        first = q * GROUPS
        copies = []
        for quadrant in range(4):
            src, base = (fp, EDGE) if quadrant < 2 else (fm, 0)
            for t in range(8):
                copies.append(
                    pltpu.make_async_copy(
                        src.at[pl.ds(base + first, GROUPS), 8 * (quadrant % 2) + t, :],
                        out.at[0, direction(quadrant, t), pl.ds(first, GROUPS), :],
                        out_sem.at[0],
                    )
                )
            src = lp if quadrant < 2 else lm
            for ct in range(4):
                copies.append(
                    pltpu.make_async_copy(
                        src.at[pl.ds(base + first, GROUPS), 2 * ct + quadrant % 2, :],
                        out.at[0, direction(quadrant, 8), pl.ds(first, GROUPS), pl.ds(128 * ct, 128)],
                        out_sem.at[0],
                    )
                )
        return copies

    for q in range(CHUNKS):
        pltpu.make_async_copy(
            ri.at[pl.ds(q * GROUPS, GROUPS)], ri.at[pl.ds(q * GROUPS, GROUPS)], back_recv.at[q]
        ).wait()

        def rows(b, _):
            block_at = q * (GROUPS // BLOCK) + b
            for j in range(BLOCK):
                r = block_at * BLOCK + j
                for ct in range(4):
                    cols = pl.ds(128 * ct, 128)
                    sea = msk[block_at + 1, j : j + 1, cols]
                    fp[r + EDGE, :, cols] += ri[r, pl.ds(MAIN * ct, 16), :].astype(F32) * sea
                    fm[r, :, cols] += ri[r, pl.ds(MAIN * ct + 16, 16), :].astype(F32) * sea
                left = ri[r, pl.ds(4 * MAIN, 16), :].astype(F32)
                lp[r + EDGE] += left[0:8] * ml[block_at + 1, j]
                lm[r] += left[8:16] * ml[block_at + 1, j]
            return 0

        lax.fori_loop(0, GROUPS // BLOCK, rows, 0)
        for copy in store_copies(q):
            copy.start()

    sent = pb.at[pl.ds(0, len(ORDER))]
    for q in range(CHUNKS):
        pltpu.make_async_copy(sent, sent, send_sem.at[q]).wait()
        pltpu.make_async_copy(sent, sent, back_send.at[q]).wait()
    for ref in (fp.at[pl.ds(EDGE, ROWS)], fm.at[pl.ds(0, ROWS)], lp.at[pl.ds(EDGE, ROWS)], lm.at[pl.ds(0, ROWS)]):
        pltpu.make_async_copy(ref, ref, out_sem.at[0]).wait()


def ordered(values):
    parts = values.reshape(NFREQ, 4, 9)
    main = parts[:, :, :8].reshape(-1)
    left = jnp.transpose(parts[:, :, 8].reshape(NFREQ, 2, 2), (2, 0, 1)).reshape(-1)
    return jnp.concatenate([main, left])


def local(spectrum, sea_mask, point_index, band_counts, sub_counts, mix_in, mix_out, growth, damping):
    freq = lax.axis_index("comp").astype(F32)
    steps = sub_counts[0]
    speed = 1.4 * jnp.power(jnp.float32(0.93), freq)
    active = (steps > jnp.arange(NSUB)).astype(F32)
    scal = speed * active / steps.astype(F32)
    raw = np.power(np.float64(1.1), np.arange(NFREQ))
    weight = np.repeat(raw / (NDIR * raw.sum()), NDIR).astype(np.float32)
    nat = np.asarray(natural_np())
    weight = weight[nat]
    high = weight.astype(jnp.bfloat16)
    low = (weight - high.astype(np.float32)).astype(jnp.bfloat16)
    mean_w = np.zeros((HID - K, K), jnp.bfloat16)
    mean_w[0], mean_w[1] = high, low
    gain = jnp.broadcast_to(0.5 * ordered(growth)[:, None], (K, 128))
    damp = jnp.broadcast_to(0.5 * ordered(damping)[:, None], (K, 128))
    hbm, vmem = pl.BlockSpec(memory_space=pl.ANY), pl.BlockSpec(memory_space=pltpu.VMEM)
    smem = pl.BlockSpec(memory_space=pltpu.SMEM)
    dma, VM = pltpu.SemaphoreType.DMA, pltpu.VMEM
    return pl.pallas_call(
        kernel,
        name="wave_step",
        out_shape=jax.ShapeDtypeStruct(spectrum.shape, F32),
        in_specs=[hbm, vmem, smem, vmem, hbm, hbm, vmem, vmem, vmem],
        out_specs=hbm,
        scratch_shapes=[
            VM((SIDE, 16, LON), F32), VM((SIDE, 16, LON), F32), VM((SIDE, 8, 128), F32), VM((SIDE, 8, 128), F32),
            VM((14, 8, LON), F32), VM((2, 8, LON), jnp.int32),
            VM((14, 8, LON), F32), VM((14, 8, LON), F32), VM((14, 8, LON), F32), VM((14, 8, LON), F32),
            VM((2, 14, 8, 8, 128), F32), VM((2, 14, 8, 8, 128), F32), VM((14, 8, 8, 128), F32),
            VM((ROWS, MSG, 128), BF16), VM((CHUNKS, GROUPS, MSG, 128), BF16),
            VM((CHUNKS, GROUPS, MSG, 128), BF16), VM((ROWS, MSG, 128), BF16),
            VM((K, K), BF16), VM((K, K), BF16), VM((K, K), BF16), VM((HID, K), BF16), VM((K, HID), BF16),
            VM((HID, LON), BF16), VM((8, LON), F32), VM((16 * GROUPS, 128), F32), VM((128, LON), BF16),
            VM((16 * GROUPS, 128), F32),
            dma((4,)), dma((2, 2)), dma((2, 2)), dma((2,)), dma((2,)), dma((1,)), dma((2,)), dma((1,)),
            dma((CHUNKS,)), dma((CHUNKS,)), dma((CHUNKS,)), dma((CHUNKS,)), dma((1,)),
        ],
        compiler_params=pltpu.CompilerParams(
            collective_id=0, has_side_effects=True, vmem_limit_bytes=60 * 1024 * 1024
        ),
    )(spectrum, sea_mask, scal, jnp.asarray(angle_tables()), mix_in, mix_out, jnp.asarray(mean_w), gain, damp)


def natural_np():
    c = np.arange(K)
    k = c & 31
    main = 36 * (c >> 5) + 9 * (k >> 3) + (k & 7)
    r = c - 1024
    left = 36 * ((r & 63) >> 1) + 9 * (2 * (r & 1) + (r >> 6)) + 8
    return np.where(c < 1024, main, left)


def solution(mesh):
    return jax.shard_map(
        local,
        mesh=mesh,
        in_specs=(
            P("comp", None, "lat", None),
            P("lat", None),
            P("lat", None),
            P("lat"),
            P("comp"),
            P(),
            P(),
            P(),
            P(),
        ),
        out_specs=P("comp", None, "lat", None),
        check_vma=False,
    )
```

```python
import functools
import math

import jax
import jax.numpy as jnp
import numpy as np
from jax import lax
from jax.experimental import pallas as pl
from jax.experimental.pallas import tpu as pltpu
from jax.sharding import PartitionSpec as P

MESH = pl.DeviceIdType.MESH
F32, BF16 = jnp.float32, jnp.bfloat16
NSUB = 4
NDIR, NFREQ, ROWS, LON = 36, 32, 96, 512
K = NDIR * NFREQ
GROUPS = 32
CHUNKS = ROWS // GROUPS
HALO = 4
EDGE = 8
SIDE = ROWS + 2 * EDGE
PHASES = (1, 2, 0)
MAIN = 32
MSG = 4 * MAIN + 16
HID = 1184
TILE1 = HID // 2
TILE2 = 512
BLOCK = 8

LATIN = [((i + dy) % 4, dy) for i in range(4) for dy in (1, 3, 2, 0) if ((i + dy) % 4, dy) != (0, 0)]
ORDER = [(dz, dy, dc) for dz, dy in LATIN for dc in (0, 1)] + [(0, 0, 1)]


def direction(quadrant, place):
    return 9 * quadrant + place


def angle_tables():
    main = [direction(q, t) for q in range(4) for t in range(8)]
    left_plus = [direction(i, 8) for _ in range(4) for i in range(2)]
    left_minus = [direction(2 + i, 8) for _ in range(4) for i in range(2)]
    angles = (np.array(main + left_plus + left_minus, np.float32) + np.float32(0.5)) * np.float32(2.0 * np.pi / NDIR)
    table = np.stack([np.abs(np.cos(angles)), np.abs(np.sin(angles))]).astype(np.float32)
    return np.ascontiguousarray(np.broadcast_to(table[:, :, None], (2, 48, 128)))


def component(c, where=jnp.where):
    k, r = c & 31, c - 1024
    left = c >= 1024
    freq = where(left, (r & 63) >> 1, c >> 5)
    turn = where(left, 9 * (2 * (r & 1) + (r >> 6)) + 8, 9 * (k >> 3) + (k & 7))
    return freq, turn


def natural(c, where=jnp.where):
    freq, turn = component(c, where)
    return NDIR * freq + turn


def first_row(side, q):
    return EDGE + q * GROUPS + (EDGE if q else 0) if side == 0 else q * GROUPS + (EDGE if q == 2 else 0)


def kernel(
    spec, mask, counts, speed, table, w_in, w_out, mean_w, growth, damping,
    out,
    fp, fm, lp, lm, mk, tb, msk, mh, ox, oxm, oy, oym, oxl, oyl, ml, flow, flow_l,
    pb, rm, ib, ri, win, wout, perm, wi, wo, gr, dp, gain, damp, sq, hq, lf, rl, tl,
    in_sem, small_sem, halo_send, halo_recv, mask_send, mask_recv, w_sem,
    send_sem, recv_sem, back_send, back_recv, out_sem,
):
    me, lat = lax.axis_index("comp"), lax.axis_index("lat")
    z, y, core = lax.div(me, 8), lax.rem(lax.div(me, 2), 4), lax.rem(me, 2)
    partners = [
        (lax.rem(z + dz, 4) * 4 + lax.rem(y + dy, 4)) * 2 + lax.rem(core + dc, 2) for dz, dy, dc in ORDER
    ]
    fields, lefts = (fp, fm), (lp, lm)

    small = [
        pltpu.make_async_copy(src, dst, small_sem.at[i])
        for i, (src, dst) in enumerate(((mask, mk), (table, tb), (growth, gr), (damping, dp)))
    ]
    small[0].start()
    small[1].start()

    spans = {1: ((24, 40), (32, 40)), 2: ((64, 32), (64, 32)), 0: ((0, 32), (0, 32))}

    def landing(side, q):
        row, rows = spans[q][side]
        return row, pl.ds(first_row(side, q) - (EDGE if q == 1 and side == 0 else 0), rows), rows

    def load(q):
        for quadrant in range(4):
            side, i = divmod(quadrant, 2)
            row, there, rows = landing(side, q)
            for t in range(8):
                pltpu.make_async_copy(
                    spec.at[0, direction(quadrant, t), pl.ds(row, rows)], fields[side].at[there, 8 * i + t, :],
                    in_sem.at[q, side],
                ).start()
            for ct in range(4):
                pltpu.make_async_copy(
                    spec.at[0, direction(quadrant, 8), pl.ds(row, rows), pl.ds(128 * ct, 128)],
                    lefts[side].at[there, 2 * ct + i, :],
                    in_sem.at[q, 2 + side],
                ).start()

    def loaded(q):
        for side in range(2):
            _, there, _ = landing(side, q)
            for ref, sem in ((fields[side], side), (lefts[side], 2 + side)):
                pltpu.make_async_copy(ref.at[there], ref.at[there], in_sem.at[q, sem]).wait()

    load(1)

    barrier = pltpu.get_barrier_semaphore()
    for partner in partners:
        pl.semaphore_signal(barrier, inc=1, device_id=(partner, lat), device_id_type=MESH)
    inner_low, inner_high = lat > 0, lat < 3

    @pl.when(inner_low)
    def _():
        pl.semaphore_signal(barrier, inc=1, device_id=(me, lat - 1), device_id_type=MESH)

    @pl.when(inner_high)
    def _():
        pl.semaphore_signal(barrier, inc=1, device_id=(me, lat + 1), device_id_type=MESH)

    load(2)
    load(0)
    w_copies = [
        pltpu.make_async_copy(w_in, win, w_sem.at[0]),
        pltpu.make_async_copy(w_out, wout, w_sem.at[1]),
        pltpu.make_async_copy(mean_w, wi.at[pl.ds(K, HID - K)], w_sem.at[2]),
    ]
    for copy in w_copies:
        copy.start()
    small[2].start()
    small[3].start()

    lane = lax.broadcasted_iota(jnp.int32, (8, 128), 1)
    sub = lax.broadcasted_iota(jnp.int32, (8, 128), 0)
    odd = lax.rem(sub, 2) == 1
    wide_sub = lax.broadcasted_iota(jnp.int32, (8, LON), 0)
    wide_lane = lax.broadcasted_iota(jnp.int32, (8, LON), 1)

    def open_lon(b):
        here = msk[b]
        ox[b] = jnp.where(wide_lane < LON - 1, here * pltpu.roll(here, LON - 1, 1), 0.0)
        oxm[b] = jnp.where(wide_lane > 0, here * pltpu.roll(here, 1, 1), 0.0)

    def open_up(b):
        oy[b] = msk[b] * jnp.where(wide_sub == 7, pltpu.roll(msk[b + 1], 7, 0), pltpu.roll(msk[b], 7, 0))

    def open_down(b):
        oym[b] = msk[b] * jnp.where(wide_sub == 0, pltpu.roll(msk[b - 1], 1, 0), pltpu.roll(msk[b], 1, 0))

    def stacked(ref, b, j):
        part = [ref[b, j : j + 1, 128 * ct : 128 * ct + 128] for ct in range(4)]
        return jnp.where(sub < 4, jnp.where(sub < 2, part[0], part[1]), jnp.where(sub < 6, part[2], part[3]))

    def left_lon(b):
        for j in range(BLOCK):
            right, leftward = stacked(ox, b, j), stacked(oxm, b, j)
            oxl[0, b, j] = jnp.where(odd, leftward, right)
            oxl[1, b, j] = jnp.where(odd, right, leftward)
            ml[b, j] = stacked(msk, b, j)

    def left_up(b):
        for j in range(BLOCK):
            oyl[0, b, j] = stacked(oy, b, j)

    def left_down(b):
        for j in range(BLOCK):
            oyl[1, b, j] = stacked(oym, b, j)

    small[0].wait()
    msk[pl.ds(1, 12)] = mk[...].astype(F32).reshape(12, 8, LON)

    def inner_openings(b, _):
        open_lon(b)
        open_up(b)
        open_down(b)
        left_lon(b)
        left_up(b)
        left_down(b)
        return 0

    lax.fori_loop(2, 12, inner_openings, 0)
    small[1].wait()
    steps = jnp.full((8, 128), counts[0], jnp.int32)
    rate = jnp.full((8, 128), speed[me], F32) / steps.astype(F32)

    flow[0] = jnp.zeros((2, NSUB, 16, LON), F32)
    flow_l[0] = jnp.zeros((2, NSUB, 8, 128), F32)

    def wide(v):
        return jnp.concatenate([v] * 4, axis=1)

    def propagate(q, side, substep):
        field, left = fields[side], lefts[side]
        a = jnp.where(steps > substep, rate, 0.0)
        coef = [
            (wide(a * tb[0, pl.ds(16 * side + 8 * g, 8), :]), wide(a * tb[1, pl.ds(16 * side + 8 * g, 8), :]))
            for g in range(2)
        ]
        coef_l = (a * tb[0, pl.ds(32 + 8 * side, 8), :], a * tb[1, pl.ds(32 + 8 * side, 8), :])
        open_y = oym if side else oy
        run_up = q == 1 or q == 2 * side
        first = first_row(side, q) // BLOCK
        low = first - (1 if run_up and side == 0 else 0)
        high = first + GROUPS // BLOCK + (1 if run_up and side == 1 else 0)
        if side == 0:
            ahead = 0 if q == 0 else -1
        else:
            ahead = 0 if q == 2 else 1

        def block(n, carry):
            flows = list(carry)
            b = high - 1 - n if side else low + n
            for step in range(BLOCK):
                j = BLOCK - 1 - step if side else step
                i = b * BLOCK + j
                e = (b + ahead, j)
                row = (b + ahead, slice(j, j + 1), slice(None))
                oy_row = open_y[row]
                for g in range(2):
                    right = g == side
                    x = field[i, pl.ds(8 * g, 8), :]
                    if substep == 0:
                        x = x * msk[row]
                    o = x * coef[g][0] * (ox if right else oxm)[row]
                    p = x * coef[g][1] * oy_row
                    inflow = pltpu.roll(o, 1 if right else LON - 1, 1)
                    field[i, pl.ds(8 * g, 8), :] = x - o + inflow - p + flows[g]
                    flows[g] = p
                x = left[i]
                if substep == 0:
                    x = x * ml[e]
                o = x * coef_l[0] * oxl[(side, *e)]
                p = x * coef_l[1] * oyl[(side, *e)]
                up = pltpu.roll(o, 1, 1)
                up = jnp.where(lane == 0, pltpu.roll(up, 2, 0), up)
                down = pltpu.roll(o, 127, 1)
                down = jnp.where(lane == 127, pltpu.roll(down, 6, 0), down)
                inflow = jnp.where(odd, down, up) if side == 0 else jnp.where(odd, up, down)
                left[i] = x - o + inflow - p + flows[2]
                flows[2] = p
            return tuple(flows)

        slot = 0 if run_up else 1
        start = (flow[slot, side, substep, 0:8], flow[slot, side, substep, 8:16], flow_l[slot, side, substep])
        end = lax.fori_loop(0, high - low, block, start)
        if q == 1:
            flow[1, side, substep, 0:8] = end[0]
            flow[1, side, substep, 8:16] = end[1]
            flow_l[1, side, substep] = end[2]

    def passes(q):
        for substep in range(NSUB):
            for side in range(2):
                propagate(q, side, substep)

    def mask_copy(up):
        return pltpu.make_async_remote_copy(
            mk.at[pl.ds(88, 8)] if up else mk.at[pl.ds(0, 8)],
            mh.at[0 if up else 1],
            mask_send.at[0 if up else 1],
            mask_recv.at[0 if up else 1],
            device_id=(me, lat + 1 if up else lat - 1),
            device_id_type=MESH,
        )

    def halo_copies(up):
        side = 0 if up else 1
        src, dst = (SIDE - HALO, EDGE - HALO) if up else (0, SIDE - EDGE)
        return [
            pltpu.make_async_remote_copy(
                ref.at[pl.ds(src, HALO)], ref.at[pl.ds(dst, HALO)], halo_send.at[side, i], halo_recv.at[side, i],
                device_id=(me, lat + 1 if up else lat - 1), device_id_type=MESH,
            )
            for i, ref in enumerate((fields[side], lefts[side]))
        ]

    def edge_copies(up):
        return [mask_copy(up), *halo_copies(up)]

    for side, at in ((0, 0), (1, SIDE - HALO)):
        fields[side][pl.ds(at, HALO)] = jnp.zeros((HALO, 16, LON), F32)
        lefts[side][pl.ds(at, HALO)] = jnp.zeros((HALO, 8, 128), F32)

    loaded(1)
    passes(1)
    neighbours = jnp.where(inner_low, 1, 0) + jnp.where(inner_high, 1, 0)
    pl.semaphore_wait(barrier, len(ORDER) + neighbours)
    loaded(2)
    loaded(0)

    @pl.when(inner_high)
    def _():
        for copy in edge_copies(True):
            copy.start()

    @pl.when(inner_low)
    def _():
        for copy in edge_copies(False):
            copy.start()

    def points(q):
        low, high = first_row(0, q), first_row(1, q)

        def row(j, _):
            r = q * GROUPS + j
            for ct in range(4):
                cols = pl.ds(128 * ct, 128)
                pb[r, pl.ds(MAIN * ct, 16), :] = fp[low + j, :, cols].astype(BF16)
                pb[r, pl.ds(MAIN * ct + 16, 16), :] = fm[high + j, :, cols].astype(BF16)
            pb[r, pl.ds(4 * MAIN, 16), :] = jnp.concatenate([lp[low + j], lm[high + j]], axis=0).astype(BF16)
            return 0

        lax.fori_loop(0, GROUPS, row, 0)

    def send_copy(q, partner):
        return pltpu.make_async_remote_copy(
            pb.at[q * GROUPS + partner], rm.at[q, me], send_sem.at[q], recv_sem.at[q],
            device_id=(partner, lat), device_id_type=MESH,
        )

    def back_copy(q, partner):
        return pltpu.make_async_remote_copy(
            ib.at[q, partner], ri.at[q * GROUPS + me], back_send.at[q], back_recv.at[q],
            device_id=(partner, lat), device_id_type=MESH,
        )

    def send(q):
        points(q)
        for partner in partners:
            send_copy(q, partner).start()
        pltpu.make_async_copy(pb.at[q * GROUPS + me], rm.at[q, me], recv_sem.at[q]).start()

    send(1)

    def select_columns(i, _):
        rows = pl.ds(pl.multiple_of(i * 384, 384), 384)
        wi[rows, :] = jnp.dot(win[rows, :], perm[...], preferred_element_type=F32).astype(BF16)
        return 0

    def select_rows(i, _):
        rows = pl.ds(pl.multiple_of(i * 384, 384), 384)
        wo[rows, pl.ds(0, K)] = jnp.dot(perm[rows, :], wout[...], preferred_element_type=F32).astype(BF16)
        return 0

    def build(across):
        def tile(i, _):
            start = pl.multiple_of(i * 128, 128)
            rows = start + lax.broadcasted_iota(jnp.int32, (128, K), 0)
            cols = lax.broadcasted_iota(jnp.int32, (128, K), 1)
            hit = natural(cols) == rows if across else natural(rows) == cols
            perm[pl.ds(start, 128), :] = jnp.where(hit, 1.0, 0.0).astype(BF16)
            return 0

        lax.fori_loop(0, K // 128, tile, 0)

    for copy in w_copies:
        copy.wait()
    build(True)
    lax.fori_loop(0, 3, select_columns, 0)

    @pl.when(inner_low)
    def _():
        for copy in edge_copies(True):
            copy.wait_recv()

    @pl.when(inner_high)
    def _():
        for copy in edge_copies(False):
            copy.wait_recv()

    @pl.when(inner_high)
    def _():
        for copy in edge_copies(True):
            copy.wait_send()

    @pl.when(inner_low)
    def _():
        for copy in edge_copies(False):
            copy.wait_send()

    @pl.when(jnp.logical_not(inner_low))
    def _():
        mh[0] = jnp.zeros((8, LON), jnp.int32)
        fp[pl.ds(HALO, HALO)] = jnp.zeros((HALO, 16, LON), F32)
        lp[pl.ds(HALO, HALO)] = jnp.zeros((HALO, 8, 128), F32)

    @pl.when(jnp.logical_not(inner_high))
    def _():
        mh[1] = jnp.zeros((8, LON), jnp.int32)
        fm[pl.ds(SIDE - EDGE, HALO)] = jnp.zeros((HALO, 16, LON), F32)
        lm[pl.ds(SIDE - EDGE, HALO)] = jnp.zeros((HALO, 8, 128), F32)

    msk[0] = mh[0].astype(F32)
    msk[13] = mh[1].astype(F32)
    for b in (0, 1, 12, 13):
        open_lon(b)
        left_lon(b)
    for b in (0, 1, 12):
        open_up(b)
        left_up(b)
    for b in (1, 12, 13):
        open_down(b)
        left_down(b)

    for q in PHASES[1:]:
        passes(q)
        send(q)

    build(False)
    lax.fori_loop(0, 3, select_rows, 0)
    wo[:, pl.ds(K, HID - K)] = jnp.zeros((K, HID - K), BF16)

    small[2].wait()
    small[3].wait()

    def rates(i, _):
        start = pl.multiple_of(i * 128, 128)
        place = start + lax.broadcasted_iota(jnp.int32, (128, NFREQ), 0)
        freq, _ = component(place)
        pick = jnp.where(freq == lax.broadcasted_iota(jnp.int32, (128, NFREQ), 1), 0.5, 0.0)
        _, turn = component(start + lax.broadcasted_iota(jnp.int32, (128, NDIR), 0))
        hit = turn == lax.broadcasted_iota(jnp.int32, (128, NDIR), 1)
        for src, dst in ((gr, gain), (dp, damp)):
            rows = jnp.dot(pick, src[...], preferred_element_type=F32, precision=lax.Precision.HIGHEST)
            picked = jnp.sum(jnp.where(hit, rows, 0.0), axis=1, keepdims=True)
            dst[pl.ds(start, 128), :] = jnp.broadcast_to(picked, (128, 128))
        return 0

    lax.fori_loop(0, K // 128, rates, 0)

    def sources(q):
        lf[...] = rm[q, :, pl.ds(4 * MAIN, 16), :].reshape(16 * GROUPS, 128).astype(F32)
        for ct in range(4):
            for i in range(2):
                rl[pl.ds(64 * i, 64), pl.ds(128 * ct, 128)] = lf[pl.ds(2 * ct + i, 64, stride=8), :].astype(BF16)

        def right_side():
            main = [rm[q, :, pl.ds(MAIN * ct, MAIN), :].reshape(MAIN * GROUPS, 128) for ct in range(4)]
            return jnp.concatenate([jnp.concatenate(main, axis=1), rl[...]], axis=0)

        for part in range(2):
            hidden = jnp.dot(wi[pl.ds(TILE1 * part, TILE1), :], right_side(), preferred_element_type=F32)
            sq[pl.ds(TILE1 * part, TILE1), :] = (hidden * hidden).astype(BF16)
            if part == 1:
                energy = hidden[K - TILE1 : K - TILE1 + 1] + hidden[K - TILE1 + 1 : K - TILE1 + 2]
                hq[...] = jnp.broadcast_to(energy / (1.0 + energy), (8, LON))
        square = sq[...]

        def rows_of(i, _):
            base = pl.multiple_of(i * TILE2, TILE2)
            dests = TILE2 // MAIN
            transfer = jnp.dot(wo[pl.ds(base, TILE2), :], square, preferred_element_type=F32)
            for ct in range(4):
                where = (q, pl.ds(i * dests, dests), pl.ds(MAIN * ct, MAIN), slice(None))
                energy = rm[where].astype(F32).reshape(TILE2, 128)
                rate = gain[pl.ds(base, TILE2), :] - damp[pl.ds(base, TILE2), :] * hq[0:1, 128 * ct : 128 * ct + 128]
                result = energy * rate + 0.125 * transfer[:, 128 * ct : 128 * ct + 128]
                ib[where] = result.astype(BF16).reshape(dests, MAIN, 128)
            return 0

        lax.fori_loop(0, MAIN * GROUPS // TILE2, rows_of, 0)
        transfer = jnp.dot(wo[pl.ds(1024, 128), :], square, preferred_element_type=F32)
        for ct in range(4):
            cols = slice(128 * ct, 128 * ct + 128)
            rate = gain[pl.ds(1024, 128), :] - damp[pl.ds(1024, 128), :] * hq[0:1, cols]
            result = rl[:, cols].astype(F32) * rate + 0.125 * transfer[:, cols]
            for i in range(2):
                tl[pl.ds(2 * ct + i, 64, stride=8), :] = result[64 * i : 64 * i + 64]
        ib[q, :, pl.ds(4 * MAIN, 16), :] = tl[...].astype(BF16).reshape(GROUPS, 16, 128)

    def chunk(q, _):
        pltpu.make_async_copy(rm.at[q], rm.at[q], recv_sem.at[q]).wait()
        sources(q)
        for partner in partners:
            back_copy(q, partner).start()
        pltpu.make_async_copy(ib.at[q, me], ri.at[q * GROUPS + me], back_recv.at[q]).start()
        return 0

    for q in PHASES:
        chunk(q, 0)

    def store_copies(q):
        first = q * GROUPS
        copies = []
        for quadrant in range(4):
            side = quadrant // 2
            src, here = fields[side], pl.ds(first_row(side, q), GROUPS)
            for t in range(8):
                copies.append(
                    pltpu.make_async_copy(
                        src.at[here, 8 * (quadrant % 2) + t, :],
                        out.at[0, direction(quadrant, t), pl.ds(first, GROUPS), :],
                        out_sem.at[0],
                    )
                )
            src = lefts[side]
            for ct in range(4):
                copies.append(
                    pltpu.make_async_copy(
                        src.at[here, 2 * ct + quadrant % 2, :],
                        out.at[0, direction(quadrant, 8), pl.ds(first, GROUPS), pl.ds(128 * ct, 128)],
                        out_sem.at[0],
                    )
                )
        return copies

    for q in PHASES:
        low, high = first_row(0, q), first_row(1, q)
        pltpu.make_async_copy(
            ri.at[pl.ds(q * GROUPS, GROUPS)], ri.at[pl.ds(q * GROUPS, GROUPS)], back_recv.at[q]
        ).wait()

        def rows(b, _):
            block_at = q * (GROUPS // BLOCK) + b + 1
            for j in range(BLOCK):
                here = b * BLOCK + j
                r = q * GROUPS + here
                for ct in range(4):
                    cols = pl.ds(128 * ct, 128)
                    sea = msk[block_at, j : j + 1, cols]
                    fp[low + here, :, cols] += ri[r, pl.ds(MAIN * ct, 16), :].astype(F32) * sea
                    fm[high + here, :, cols] += ri[r, pl.ds(MAIN * ct + 16, 16), :].astype(F32) * sea
                left = ri[r, pl.ds(4 * MAIN, 16), :].astype(F32)
                lp[low + here] += left[0:8] * ml[block_at, j]
                lm[high + here] += left[8:16] * ml[block_at, j]
            return 0

        lax.fori_loop(0, GROUPS // BLOCK, rows, 0)
        for copy in store_copies(q):
            copy.start()

    sent = pb.at[pl.ds(0, len(ORDER))]
    for q in range(CHUNKS):
        pltpu.make_async_copy(sent, sent, send_sem.at[q]).wait()
        pltpu.make_async_copy(sent, sent, back_send.at[q]).wait()
    for ref in (fp.at[pl.ds(0, ROWS)], fm.at[pl.ds(0, ROWS)], lp.at[pl.ds(0, ROWS)], lm.at[pl.ds(0, ROWS)]):
        pltpu.make_async_copy(ref, ref, out_sem.at[0]).wait()


def local(spectrum, sea_mask, point_index, band_counts, sub_counts, mix_in, mix_out, growth, damping):
    speed = (1.4 * np.power(np.float64(0.93), np.arange(NFREQ))).astype(np.float32)
    raw = np.power(np.float64(1.1), np.arange(NFREQ))
    weight = np.repeat(raw / (NDIR * raw.sum()), NDIR).astype(np.float32)
    weight = weight[natural(np.arange(K), np.where)]
    high = weight.astype(jnp.bfloat16)
    low = (weight - high.astype(np.float32)).astype(jnp.bfloat16)
    mean_w = np.zeros((HID - K, K), jnp.bfloat16)
    mean_w[0], mean_w[1] = high, low
    hbm, smem = pl.BlockSpec(memory_space=pl.ANY), pl.BlockSpec(memory_space=pltpu.SMEM)
    dma, VM = pltpu.SemaphoreType.DMA, pltpu.VMEM
    masks = [VM((14, 8, LON), F32)]
    return pl.pallas_call(
        kernel,
        name="wave_step",
        out_shape=jax.ShapeDtypeStruct(spectrum.shape, F32),
        in_specs=[hbm, hbm, smem, smem, hbm, hbm, hbm, hbm, hbm, hbm],
        out_specs=hbm,
        scratch_shapes=[
            VM((SIDE, 16, LON), F32), VM((SIDE, 16, LON), F32), VM((SIDE, 8, 128), F32), VM((SIDE, 8, 128), F32),
            VM((ROWS, LON), jnp.int32), VM((2, 48, 128), F32), *masks, VM((2, 8, LON), jnp.int32), *masks * 4,
            VM((2, 14, 8, 8, 128), F32), VM((2, 14, 8, 8, 128), F32), VM((14, 8, 8, 128), F32),
            VM((2, 2, NSUB, 16, LON), F32), VM((2, 2, NSUB, 8, 128), F32),
            VM((ROWS, MSG, 128), BF16), VM((CHUNKS, GROUPS, MSG, 128), BF16),
            VM((CHUNKS, GROUPS, MSG, 128), BF16), VM((ROWS, MSG, 128), BF16),
            VM((K, K), BF16), VM((K, K), BF16), VM((K, K), BF16), VM((HID, K), BF16), VM((K, HID), BF16),
            VM((NFREQ, NDIR), F32), VM((NFREQ, NDIR), F32), VM((K, 128), F32), VM((K, 128), F32),
            VM((HID, LON), BF16), VM((8, LON), F32), VM((16 * GROUPS, 128), F32), VM((128, LON), BF16),
            VM((16 * GROUPS, 128), F32),
            dma((CHUNKS, 4)), dma((4,)), dma((2, 2)), dma((2, 2)), dma((2,)), dma((2,)), dma((3,)),
            dma((CHUNKS,)), dma((CHUNKS,)), dma((CHUNKS,)), dma((CHUNKS,)), dma((1,)),
        ],
        compiler_params=pltpu.CompilerParams(
            collective_id=0, has_side_effects=True, vmem_limit_bytes=60 * 1024 * 1024
        ),
    )(spectrum, sea_mask, sub_counts, jnp.asarray(speed), jnp.asarray(angle_tables()), mix_in, mix_out,
      jnp.asarray(mean_w), growth, damping)


def solution(mesh):
    return jax.shard_map(
        local,
        mesh=mesh,
        in_specs=(
            P("comp", None, "lat", None),
            P("lat", None),
            P("lat", None),
            P("lat"),
            P("comp"),
            P(),
            P(),
            P(),
            P(),
        ),
        out_specs=P("comp", None, "lat", None),
        check_vma=False,
    )
```

```python
import functools
import math

import jax
import jax.numpy as jnp
import numpy as np
from jax import lax
from jax.experimental import pallas as pl
from jax.experimental.pallas import tpu as pltpu
from jax.sharding import PartitionSpec as P

MESH = pl.DeviceIdType.MESH
F32, BF16 = jnp.float32, jnp.bfloat16
NSUB = 4
VMEM = 67_043_328
NDIR, NFREQ, ROWS, LON = 36, 32, 96, 512
K = NDIR * NFREQ
GROUPS = 32
CHUNKS = ROWS // GROUPS
HALO = 4
PHASES = (1, 2, 0)
PIECES = ((32, 16), (48, 16), (64, 32), (0, 32))
FIELD_BYTES = ROWS * (2 * 16 * LON + 2 * 8 * 128) * 4
MAIN = 32
MSG = 4 * MAIN + 16
HID = 1184
TILE1 = HID // 2
TILE2 = 512
BLOCK = 8

LATIN = [((i + dy) % 4, dy) for i in range(4) for dy in (1, 3, 2, 0) if ((i + dy) % 4, dy) != (0, 0)]


def direction(quadrant, place):
    return 9 * quadrant + place


def angle_tables():
    main = [direction(q, t) for q in range(4) for t in range(8)]
    left_plus = [direction(i, 8) for _ in range(4) for i in range(2)]
    left_minus = [direction(2 + i, 8) for _ in range(4) for i in range(2)]
    angles = (np.array(main + left_plus + left_minus, np.float32) + np.float32(0.5)) * np.float32(2.0 * np.pi / NDIR)
    table = np.stack([np.abs(np.cos(angles)), np.abs(np.sin(angles))]).astype(np.float32)
    return np.ascontiguousarray(np.broadcast_to(table[:, :, None], (2, 48, 128)))


def component(c, where=jnp.where):
    k, r = c & 31, c - 1024
    left = c >= 1024
    freq = where(left, (r & 63) >> 1, c >> 5)
    turn = where(left, 9 * (2 * (r & 1) + (r >> 6)) + 8, 9 * (k >> 3) + (k & 7))
    return freq, turn


def natural(c, where=jnp.where):
    freq, turn = component(c, where)
    return NDIR * freq + turn


def kernel(
    spec, mask, counts, speed, table, w_in, w_out, mean_w, growth, damping,
    fp, fm, lp, lm,
    run, run_l, mk, tb, msk, mh, ox, oxm, oy, oym, oxl, oyl, ml, flow, flow_l,
    pb, rm, ib, ri, win, wout, perm, wi, wo, gr, dp, gain, damp, sq, hq, lf, rl, tl,
    in_sem, small_sem, halo_send, halo_recv, mask_send, mask_recv, w_sem,
    send_sem, recv_sem, back_send, back_recv,
):
    me, lat = lax.axis_index("comp"), lax.axis_index("lat")
    z, y, core = lax.div(me, 8), lax.rem(lax.div(me, 2), 4), lax.rem(me, 2)
    chip = lax.div(me, 2)
    others = [lax.rem(z + dz, 4) * 4 + lax.rem(y + dy, 4) for dz, dy in LATIN]
    fields, lefts = (fp, fm), (lp, lm)

    small = [
        pltpu.make_async_copy(src, dst, small_sem.at[i])
        for i, (src, dst) in enumerate(((mask, mk), (table, tb), (growth, gr), (damping, dp)))
    ]
    small[0].start()
    small[1].start()

    spans = ((24, 32), (56, 40), (0, 24))

    def load(n):
        rows = pl.ds(*spans[n])
        for quadrant in range(4):
            side, i = divmod(quadrant, 2)
            for t in range(8):
                pltpu.make_async_copy(
                    spec.at[0, direction(quadrant, t), rows], fields[side].at[rows, 8 * i + t, :], in_sem.at[n, side]
                ).start()
            for ct in range(4):
                pltpu.make_async_copy(
                    spec.at[0, direction(quadrant, 8), rows, pl.ds(128 * ct, 128)],
                    lefts[side].at[rows, 2 * ct + i, :],
                    in_sem.at[n, 2 + side],
                ).start()

    def loaded(n):
        rows = pl.ds(*spans[n])
        for k, ref in enumerate(fields + lefts):
            pltpu.make_async_copy(ref.at[rows], ref.at[rows], in_sem.at[n, k]).wait()

    run_ups = {(0, 0): (0, 24), (0, 1): (1, 48), (1, 1): (2, 64)}
    halo_slot = (3, 4)
    load(0)

    barrier = pltpu.get_barrier_semaphore()
    for other in others:
        for c in range(2):
            pl.semaphore_signal(barrier, inc=1, device_id=(2 * other + c, lat), device_id_type=MESH)
    pl.semaphore_signal(barrier, inc=1, device_id=(2 * chip + 1 - core, lat), device_id_type=MESH)
    inner_low, inner_high = lat > 0, lat < 3

    @pl.when(inner_low)
    def _():
        pl.semaphore_signal(barrier, inc=1, device_id=(me, lat - 1), device_id_type=MESH)

    @pl.when(inner_high)
    def _():
        pl.semaphore_signal(barrier, inc=1, device_id=(me, lat + 1), device_id_type=MESH)

    load(1)
    load(2)
    w_copies = [
        pltpu.make_async_copy(w_in, win, w_sem.at[0]),
        pltpu.make_async_copy(w_out, wout, w_sem.at[1]),
        pltpu.make_async_copy(mean_w, wi.at[pl.ds(K, HID - K)], w_sem.at[2]),
    ]
    for copy in w_copies:
        copy.start()
    small[2].start()
    small[3].start()

    lane = lax.broadcasted_iota(jnp.int32, (8, 128), 1)
    sub = lax.broadcasted_iota(jnp.int32, (8, 128), 0)
    odd = lax.rem(sub, 2) == 1
    wide_sub = lax.broadcasted_iota(jnp.int32, (8, LON), 0)
    wide_lane = lax.broadcasted_iota(jnp.int32, (8, LON), 1)

    def open_lon(b):
        here = msk[b]
        ox[b] = jnp.where(wide_lane < LON - 1, here * pltpu.roll(here, LON - 1, 1), 0.0)
        oxm[b] = jnp.where(wide_lane > 0, here * pltpu.roll(here, 1, 1), 0.0)

    def open_up(b):
        oy[b] = msk[b] * jnp.where(wide_sub == 7, pltpu.roll(msk[b + 1], 7, 0), pltpu.roll(msk[b], 7, 0))

    def open_down(b):
        oym[b] = msk[b] * jnp.where(wide_sub == 0, pltpu.roll(msk[b - 1], 1, 0), pltpu.roll(msk[b], 1, 0))

    def stacked(ref, b, j):
        part = [ref[b, j : j + 1, 128 * ct : 128 * ct + 128] for ct in range(4)]
        return jnp.where(sub < 4, jnp.where(sub < 2, part[0], part[1]), jnp.where(sub < 6, part[2], part[3]))

    def left_lon(b):
        for j in range(BLOCK):
            right, leftward = stacked(ox, b, j), stacked(oxm, b, j)
            oxl[0, b, j] = jnp.where(odd, leftward, right)
            oxl[1, b, j] = jnp.where(odd, right, leftward)
            ml[b, j] = stacked(msk, b, j)

    def left_up(b):
        for j in range(BLOCK):
            oyl[0, b, j] = stacked(oy, b, j)

    def left_down(b):
        for j in range(BLOCK):
            oyl[1, b, j] = stacked(oym, b, j)

    small[0].wait()
    msk[pl.ds(1, 12)] = mk[...].astype(F32).reshape(12, 8, LON)

    def inner_openings(b, _):
        open_lon(b)
        open_up(b)
        open_down(b)
        left_lon(b)
        left_up(b)
        left_down(b)
        return 0

    lax.fori_loop(4, 8, inner_openings, 0)
    small[1].wait()
    steps = jnp.full((8, 128), counts[0], jnp.int32)
    rate = jnp.full((8, 128), speed[me], F32) / steps.astype(F32)

    def wide(v):
        return jnp.concatenate([v] * 4, axis=1)

    def propagate(n, side, substep):
        a = jnp.where(steps > substep, rate, 0.0)
        coef = [
            (wide(a * tb[0, pl.ds(16 * side + 8 * g, 8), :]), wide(a * tb[1, pl.ds(16 * side + 8 * g, 8), :]))
            for g in range(2)
        ]
        coef_l = (a * tb[0, pl.ds(32 + 8 * side, 8), :], a * tb[1, pl.ds(32 + 8 * side, 8), :])
        open_y = oym if side else oy

        def block(field, left, base, at, places, carry, source=None):
            field_in, left_in, base_in = source or (field, left, base)
            flows = list(carry)
            for j in places:
                i = base + j
                e = (at, j)
                row = (at, slice(j, j + 1), slice(None))
                oy_row = open_y[row]
                for g in range(2):
                    right = g == side
                    x = field_in[base_in + j, pl.ds(8 * g, 8), :]
                    if substep == 0:
                        x = x * msk[row]
                    o = x * coef[g][0] * (ox if right else oxm)[row]
                    p = x * coef[g][1] * oy_row
                    inflow = pltpu.roll(o, 1 if right else LON - 1, 1)
                    field[i, pl.ds(8 * g, 8), :] = x - o + inflow - p + flows[g]
                    flows[g] = p
                x = left_in[base_in + j]
                if substep == 0:
                    x = x * ml[e]
                o = x * coef_l[0] * oxl[(side, *e)]
                p = x * coef_l[1] * oyl[(side, *e)]
                up = pltpu.roll(o, 1, 1)
                up = jnp.where(lane == 0, pltpu.roll(up, 2, 0), up)
                down = pltpu.roll(o, 127, 1)
                down = jnp.where(lane == 127, pltpu.roll(down, 6, 0), down)
                inflow = jnp.where(odd, down, up) if side == 0 else jnp.where(odd, up, down)
                left[i] = x - o + inflow - p + flows[2]
                flows[2] = p
            return tuple(flows)

        first, rows = PIECES[n]
        low, high = first // BLOCK, (first + rows) // BLOCK
        edge = 3 - side
        if n == edge or (n, side) in run_ups:
            slot = halo_slot[side] if n == edge else run_ups[n, side][0]
            zero = jnp.zeros((8, LON), F32)
            start = (zero, zero, jnp.zeros((8, 128), F32))
            places = range(HALO - 1, -1, -1) if side else range(HALO, BLOCK)
            source = None
            if substep == 0 and n != edge:
                source = (fields[side], lefts[side], run_ups[n, side][1])
            start = block(run.at[slot], run_l.at[slot], 0, high + 1 if side else low, places, start, source)
        else:
            start = (flow[side, substep, 0:8], flow[side, substep, 8:16], flow_l[side, substep])

        def main(k, carry):
            b = high - 1 - k if side else low + k
            places = range(BLOCK - 1, -1, -1) if side else range(BLOCK)
            return block(fields[side], lefts[side], b * BLOCK, b + 1, places, carry)

        end = lax.fori_loop(0, high - low, main, start)
        if n == 0 or (n == 1 and side == 0):
            flow[side, substep, 0:8] = end[0]
            flow[side, substep, 8:16] = end[1]
            flow_l[side, substep] = end[2]

    def passes(n):
        for substep in range(NSUB):
            for side in range(2):
                propagate(n, side, substep)

    def mask_copy(up):
        return pltpu.make_async_remote_copy(
            mk.at[pl.ds(88, 8)] if up else mk.at[pl.ds(0, 8)],
            mh.at[0 if up else 1],
            mask_send.at[0 if up else 1],
            mask_recv.at[0 if up else 1],
            device_id=(me, lat + 1 if up else lat - 1),
            device_id_type=MESH,
        )

    def halo_copies(up):
        side = 0 if up else 1
        src, dst = (ROWS - HALO, HALO) if up else (0, 0)
        return [
            pltpu.make_async_remote_copy(
                ref.at[pl.ds(src, HALO)], to.at[halo_slot[side], pl.ds(dst, HALO)],
                halo_send.at[side, i], halo_recv.at[side, i],
                device_id=(me, lat + 1 if up else lat - 1), device_id_type=MESH,
            )
            for i, (ref, to) in enumerate(((fields[side], run), (lefts[side], run_l)))
        ]

    def edge_copies(up):
        return [mask_copy(up), *halo_copies(up)]

    loaded(0)
    passes(0)
    neighbours = jnp.where(inner_low, 1, 0) + jnp.where(inner_high, 1, 0)
    pl.semaphore_wait(barrier, 2 * len(LATIN) + 1 + neighbours)

    def points(first, rows):
        def row(j, _):
            r = first + j
            for ct in range(4):
                cols = pl.ds(128 * ct, 128)
                pb[r, pl.ds(MAIN * ct, 16), :] = fp[r, :, cols].astype(BF16)
                pb[r, pl.ds(MAIN * ct + 16, 16), :] = fm[r, :, cols].astype(BF16)
            pb[r, pl.ds(4 * MAIN, 16), :] = jnp.concatenate([lp[r], lm[r]], axis=0).astype(BF16)
            return 0

        lax.fori_loop(0, rows, row, 0)

    def send_copy(q, to, c):
        return pltpu.make_async_remote_copy(
            pb.at[q * GROUPS + 16 * c + to], rm.at[q, me], send_sem.at[q], recv_sem.at[q],
            device_id=(2 * to + c, lat), device_id_type=MESH,
        )

    def back_copy(q, to, c):
        return pltpu.make_async_remote_copy(
            ib.at[q, 2 * to + c], ri.at[q * GROUPS + 16 * core + chip], back_send.at[q], back_recv.at[q],
            device_id=(2 * to + c, lat), device_id_type=MESH,
        )

    def send(q, c):
        for other in others:
            send_copy(q, other, c).start()

        @pl.when(core != c)
        def _():
            send_copy(q, chip, c).start()

        @pl.when(core == c)
        def _():
            pltpu.make_async_copy(pb.at[q * GROUPS + 16 * c + chip], rm.at[q, me], recv_sem.at[q]).start()

    points(*PIECES[0])
    send(1, 0)
    loaded(1)
    loaded(2)

    @pl.when(inner_high)
    def _():
        for copy in edge_copies(True):
            copy.start()

    @pl.when(inner_low)
    def _():
        for copy in edge_copies(False):
            copy.start()

    lax.fori_loop(2, 4, inner_openings, 0)
    lax.fori_loop(8, 12, inner_openings, 0)
    passes(1)
    points(*PIECES[1])
    send(1, 1)

    def select_columns(i, _):
        rows = pl.ds(pl.multiple_of(i * 384, 384), 384)
        wi[rows, :] = jnp.dot(win[rows, :], perm[...], preferred_element_type=F32).astype(BF16)
        return 0

    def select_rows(i, _):
        rows = pl.ds(pl.multiple_of(i * 384, 384), 384)
        wo[rows, pl.ds(0, K)] = jnp.dot(perm[rows, :], wout[...], preferred_element_type=F32).astype(BF16)
        return 0

    def build(across):
        def tile(i, _):
            start = pl.multiple_of(i * 128, 128)
            rows = start + lax.broadcasted_iota(jnp.int32, (128, K), 0)
            cols = lax.broadcasted_iota(jnp.int32, (128, K), 1)
            hit = natural(cols) == rows if across else natural(rows) == cols
            perm[pl.ds(start, 128), :] = jnp.where(hit, 1.0, 0.0).astype(BF16)
            return 0

        lax.fori_loop(0, K // 128, tile, 0)

    @pl.when(inner_low)
    def _():
        for copy in edge_copies(True):
            copy.wait_recv()

    @pl.when(inner_high)
    def _():
        for copy in edge_copies(False):
            copy.wait_recv()

    @pl.when(inner_high)
    def _():
        for copy in edge_copies(True):
            copy.wait_send()

    @pl.when(inner_low)
    def _():
        for copy in edge_copies(False):
            copy.wait_send()

    @pl.when(jnp.logical_not(inner_low))
    def _():
        mh[0] = jnp.zeros((8, LON), jnp.int32)
        run[halo_slot[0], pl.ds(HALO, HALO)] = jnp.zeros((HALO, 16, LON), F32)
        run_l[halo_slot[0], pl.ds(HALO, HALO)] = jnp.zeros((HALO, 8, 128), F32)

    @pl.when(jnp.logical_not(inner_high))
    def _():
        mh[1] = jnp.zeros((8, LON), jnp.int32)
        run[halo_slot[1], pl.ds(0, HALO)] = jnp.zeros((HALO, 16, LON), F32)
        run_l[halo_slot[1], pl.ds(0, HALO)] = jnp.zeros((HALO, 8, 128), F32)

    msk[0] = mh[0].astype(F32)
    msk[13] = mh[1].astype(F32)
    for b in (0, 1, 12, 13):
        open_lon(b)
        left_lon(b)
    for b in (0, 1, 12):
        open_up(b)
        left_up(b)
    for b in (1, 12, 13):
        open_down(b)
        left_down(b)

    for n, q in ((2, 2), (3, 0)):
        passes(n)
        points(*PIECES[n])
        send(q, 0)
        send(q, 1)

    for copy in w_copies:
        copy.wait()
    build(True)
    lax.fori_loop(0, 3, select_columns, 0)

    build(False)
    lax.fori_loop(0, 3, select_rows, 0)
    wo[:, pl.ds(K, HID - K)] = jnp.zeros((K, HID - K), BF16)

    small[2].wait()
    small[3].wait()

    def rates(i, _):
        start = pl.multiple_of(i * 128, 128)
        place = start + lax.broadcasted_iota(jnp.int32, (128, NFREQ), 0)
        freq, _ = component(place)
        pick = jnp.where(freq == lax.broadcasted_iota(jnp.int32, (128, NFREQ), 1), 0.5, 0.0)
        _, turn = component(start + lax.broadcasted_iota(jnp.int32, (128, NDIR), 0))
        hit = turn == lax.broadcasted_iota(jnp.int32, (128, NDIR), 1)
        for src, dst in ((gr, gain), (dp, damp)):
            rows = jnp.dot(pick, src[...], preferred_element_type=F32, precision=lax.Precision.HIGHEST)
            picked = jnp.sum(jnp.where(hit, rows, 0.0), axis=1, keepdims=True)
            dst[pl.ds(start, 128), :] = jnp.broadcast_to(picked, (128, 128))
        return 0

    lax.fori_loop(0, K // 128, rates, 0)

    def sources(q):
        lf[...] = rm[q, :, pl.ds(4 * MAIN, 16), :].reshape(16 * GROUPS, 128).astype(F32)
        for ct in range(4):
            for i in range(2):
                rl[pl.ds(64 * i, 64), pl.ds(128 * ct, 128)] = lf[pl.ds(2 * ct + i, 64, stride=8), :].astype(BF16)

        def right_side():
            main = [rm[q, :, pl.ds(MAIN * ct, MAIN), :].reshape(MAIN * GROUPS, 128) for ct in range(4)]
            return jnp.concatenate([jnp.concatenate(main, axis=1), rl[...]], axis=0)

        for part in range(2):
            hidden = jnp.dot(wi[pl.ds(TILE1 * part, TILE1), :], right_side(), preferred_element_type=F32)
            sq[pl.ds(TILE1 * part, TILE1), :] = (hidden * hidden).astype(BF16)
            if part == 1:
                energy = hidden[K - TILE1 : K - TILE1 + 1] + hidden[K - TILE1 + 1 : K - TILE1 + 2]
                hq[...] = jnp.broadcast_to(energy / (1.0 + energy), (8, LON))
        square = sq[...]

        def rows_of(i, _):
            base = pl.multiple_of(i * TILE2, TILE2)
            dests = TILE2 // MAIN
            transfer = jnp.dot(wo[pl.ds(base, TILE2), :], square, preferred_element_type=F32)
            for ct in range(4):
                where = (q, pl.ds(i * dests, dests), pl.ds(MAIN * ct, MAIN), slice(None))
                energy = rm[where].astype(F32).reshape(TILE2, 128)
                rate = gain[pl.ds(base, TILE2), :] - damp[pl.ds(base, TILE2), :] * hq[0:1, 128 * ct : 128 * ct + 128]
                result = energy * rate + 0.125 * transfer[:, 128 * ct : 128 * ct + 128]
                ib[where] = result.astype(BF16).reshape(dests, MAIN, 128)
            return 0

        lax.fori_loop(0, MAIN * GROUPS // TILE2, rows_of, 0)
        transfer = jnp.dot(wo[pl.ds(1024, 128), :], square, preferred_element_type=F32)
        for ct in range(4):
            cols = slice(128 * ct, 128 * ct + 128)
            rate = gain[pl.ds(1024, 128), :] - damp[pl.ds(1024, 128), :] * hq[0:1, cols]
            result = rl[:, cols].astype(F32) * rate + 0.125 * transfer[:, cols]
            for i in range(2):
                tl[pl.ds(2 * ct + i, 64, stride=8), :] = result[64 * i : 64 * i + 64]
        ib[q, :, pl.ds(4 * MAIN, 16), :] = tl[...].astype(BF16).reshape(GROUPS, 16, 128)

    def chunk(q):
        pltpu.make_async_copy(rm.at[q], rm.at[q], recv_sem.at[q]).wait()
        sources(q)
        for c in range(2):
            for other in others:
                back_copy(q, other, c).start()
        back_copy(q, chip, 1 - core).start()
        pltpu.make_async_copy(ib.at[q, me], ri.at[q * GROUPS + 16 * core + chip], back_recv.at[q]).start()

    for q in PHASES:
        chunk(q)

    for q in PHASES:
        pltpu.make_async_copy(
            ri.at[pl.ds(q * GROUPS, GROUPS)], ri.at[pl.ds(q * GROUPS, GROUPS)], back_recv.at[q]
        ).wait()

        def rows(b, _):
            block_at = q * (GROUPS // BLOCK) + b + 1
            for j in range(BLOCK):
                r = q * GROUPS + b * BLOCK + j
                for ct in range(4):
                    cols = pl.ds(128 * ct, 128)
                    sea = msk[block_at, j : j + 1, cols]
                    fp[r, :, cols] += ri[r, pl.ds(MAIN * ct, 16), :].astype(F32) * sea
                    fm[r, :, cols] += ri[r, pl.ds(MAIN * ct + 16, 16), :].astype(F32) * sea
                left = ri[r, pl.ds(4 * MAIN, 16), :].astype(F32)
                lp[r] += left[0:8] * ml[block_at, j]
                lm[r] += left[8:16] * ml[block_at, j]
            return 0

        lax.fori_loop(0, GROUPS // BLOCK, rows, 0)

    sent = pb.at[pl.ds(0, 2 * len(LATIN) + 1)]
    for q in range(CHUNKS):
        pltpu.make_async_copy(sent, sent, send_sem.at[q]).wait()
        pltpu.make_async_copy(sent, sent, back_send.at[q]).wait()


def store(fp, fm, lp, lm, out, sem):
    for quadrant in range(4):
        side, i = divmod(quadrant, 2)
        for t in range(8):
            pltpu.make_async_copy((fp, fm)[side].at[:, 8 * i + t, :], out.at[0, direction(quadrant, t)], sem.at[0]).start()
        for ct in range(4):
            pltpu.make_async_copy(
                (lp, lm)[side].at[:, 2 * ct + i, :], out.at[0, direction(quadrant, 8), :, pl.ds(128 * ct, 128)], sem.at[0]
            ).start()
    for ref in (fp, fm, lp, lm):
        pltpu.make_async_copy(ref, ref, sem.at[0]).wait()


def local(spectrum, sea_mask, point_index, band_counts, sub_counts, mix_in, mix_out, growth, damping):
    speed = (1.4 * np.power(np.float64(0.93), np.arange(NFREQ))).astype(np.float32)
    raw = np.power(np.float64(1.1), np.arange(NFREQ))
    weight = np.repeat(raw / (NDIR * raw.sum()), NDIR).astype(np.float32)
    weight = weight[natural(np.arange(K), np.where)]
    high = weight.astype(jnp.bfloat16)
    low = (weight - high.astype(np.float32)).astype(jnp.bfloat16)
    mean_w = np.zeros((HID - K, K), jnp.bfloat16)
    mean_w[0], mean_w[1] = high, low
    hbm, smem = pl.BlockSpec(memory_space=pl.ANY), pl.BlockSpec(memory_space=pltpu.SMEM)
    dma, VM = pltpu.SemaphoreType.DMA, pltpu.VMEM
    masks = [VM((14, 8, LON), F32)]
    fields = pl.pallas_call(
        kernel,
        name="wave_step",
        out_shape=[VM((ROWS, 16, LON), F32)] * 2 + [VM((ROWS, 8, 128), F32)] * 2,
        in_specs=[hbm, hbm, smem, smem, hbm, hbm, hbm, hbm, hbm, hbm],
        out_specs=[pl.BlockSpec(memory_space=VM)] * 4,
        scratch_shapes=[
            VM((5, BLOCK, 16, LON), F32), VM((5, BLOCK, 8, 128), F32),
            VM((ROWS, LON), jnp.int32), VM((2, 48, 128), F32), *masks, VM((2, 8, LON), jnp.int32), *masks * 4,
            VM((2, 14, 8, 8, 128), F32), VM((2, 14, 8, 8, 128), F32), VM((14, 8, 8, 128), F32),
            VM((2, NSUB, 16, LON), F32), VM((2, NSUB, 8, 128), F32),
            VM((ROWS, MSG, 128), BF16), VM((CHUNKS, GROUPS, MSG, 128), BF16),
            VM((CHUNKS, GROUPS, MSG, 128), BF16), VM((ROWS, MSG, 128), BF16),
            VM((K, K), BF16), VM((K, K), BF16), VM((K, K), BF16), VM((HID, K), BF16), VM((K, HID), BF16),
            VM((NFREQ, NDIR), F32), VM((NFREQ, NDIR), F32), VM((K, 128), F32), VM((K, 128), F32),
            VM((HID, LON), BF16), VM((8, LON), F32), VM((16 * GROUPS, 128), F32), VM((128, LON), BF16),
            VM((16 * GROUPS, 128), F32),
            dma((3, 4)), dma((4,)), dma((2, 2)), dma((2, 2)), dma((2,)), dma((2,)), dma((3,)),
            dma((CHUNKS,)), dma((CHUNKS,)), dma((CHUNKS,)), dma((CHUNKS,)),
        ],
        compiler_params=pltpu.CompilerParams(
            collective_id=0, has_side_effects=True, vmem_limit_bytes=VMEM - FIELD_BYTES
        ),
    )(spectrum, sea_mask, sub_counts, jnp.asarray(speed), jnp.asarray(angle_tables()), mix_in, mix_out,
      jnp.asarray(mean_w), growth, damping)
    return pl.pallas_call(
        store,
        name="wave_store",
        out_shape=jax.ShapeDtypeStruct(spectrum.shape, F32),
        in_specs=[pl.BlockSpec(memory_space=VM)] * 4,
        out_specs=hbm,
        scratch_shapes=[dma((1,))],
        compiler_params=pltpu.CompilerParams(vmem_limit_bytes=1024 * 1024),
    )(*[pltpu.with_memory_space_constraint(field, VM) for field in fields])


def solution(mesh):
    return jax.shard_map(
        local,
        mesh=mesh,
        in_specs=(
            P("comp", None, "lat", None),
            P("lat", None),
            P("lat", None),
            P("lat"),
            P("comp"),
            P(),
            P(),
            P(),
            P(),
        ),
        out_specs=P("comp", None, "lat", None),
        check_vma=False,
    )
```

```python
import functools
import math

import jax
import jax.numpy as jnp
import numpy as np
from jax import lax
from jax.experimental import pallas as pl
from jax.experimental.pallas import tpu as pltpu
from jax.sharding import PartitionSpec as P

MESH = pl.DeviceIdType.MESH
F32, BF16 = jnp.float32, jnp.bfloat16
NSUB = 4
VMEM = 67_043_328
NDIR, NFREQ, ROWS, LON = 36, 32, 96, 512
K = NDIR * NFREQ
GROUPS = 32
CHUNKS = ROWS // GROUPS
HALO = 4
PHASES = (1, 2, 0)
PIECES = (32, 48, 64, 16, 80, 0)
PIECE = 16
FIELD_BYTES = ROWS * (2 * 16 * LON + 2 * 8 * 128) * 4
MAIN = 32
PART = 64
MSG = 2 * PART + 16
HID = 1184
TILE1 = HID // 2
TILE2 = 512
BLOCK = 8

LATIN = [((i + dy) % 4, dy) for i in range(4) for dy in (1, 3, 2, 0) if ((i + dy) % 4, dy) != (0, 0)]


def direction(quadrant, place):
    return 9 * quadrant + place


def angle_tables():
    main = [direction(q, t) for q in range(4) for t in range(8)]
    left_plus = [direction(i, 8) for _ in range(4) for i in range(2)]
    left_minus = [direction(2 + i, 8) for _ in range(4) for i in range(2)]
    angles = (np.array(main + left_plus + left_minus, np.float32) + np.float32(0.5)) * np.float32(2.0 * np.pi / NDIR)
    table = np.stack([np.abs(np.cos(angles)), np.abs(np.sin(angles))]).astype(np.float32)
    return np.ascontiguousarray(np.broadcast_to(table[:, :, None], (2, 48, 128)))


def component(c, where=jnp.where):
    k, r = c & 31, c - 1024
    left = c >= 1024
    freq = where(left, (r & 63) >> 1, c >> 5)
    turn = where(left, 9 * (2 * (r & 1) + (r >> 6)) + 8, 9 * (k >> 3) + (k & 7))
    return freq, turn


def natural(c, where=jnp.where):
    freq, turn = component(c, where)
    return NDIR * freq + turn


def kernel(
    spec, mask, counts, speed, table, w_in, w_out, mean_w, growth, damping,
    fp, fm, lp, lm,
    run, run_l, mk, tb, msk, mh, ox, oxm, oy, oym, oxl, oyl, ml, flow, flow_l,
    pb, rm, ib, ri, win, wout, perm, wi, wo, gr, dp, gain, damp, sq, hq, lf, rl, tl,
    in_sem, small_sem, halo_send, halo_recv, mask_send, mask_recv, w_sem,
    send_sem, recv_sem, back_send, back_recv,
):
    me, lat = lax.axis_index("comp"), lax.axis_index("lat")
    z, y, core = lax.div(me, 8), lax.rem(lax.div(me, 2), 4), lax.rem(me, 2)
    chip = lax.div(me, 2)
    others = [lax.rem(z + dz, 4) * 4 + lax.rem(y + dy, 4) for dz, dy in LATIN]
    fields, lefts = (fp, fm), (lp, lm)

    small = [
        pltpu.make_async_copy(src, dst, small_sem.at[i])
        for i, (src, dst) in enumerate(((mask, mk), (table, tb), (growth, gr), (damping, dp)))
    ]
    small[0].start()
    small[1].start()

    spans = ((24, 32), (56, 40), (0, 24))

    def load(n):
        rows = pl.ds(*spans[n])
        for quadrant in range(4):
            side, i = divmod(quadrant, 2)
            for t in range(8):
                pltpu.make_async_copy(
                    spec.at[0, direction(quadrant, t), rows], fields[side].at[rows, 8 * i + t, :], in_sem.at[n, side]
                ).start()
            for ct in range(4):
                pltpu.make_async_copy(
                    spec.at[0, direction(quadrant, 8), rows, pl.ds(128 * ct, 128)],
                    lefts[side].at[rows, 2 * ct + i, :],
                    in_sem.at[n, 2 + side],
                ).start()

    def loaded(n):
        rows = pl.ds(*spans[n])
        for k, ref in enumerate(fields + lefts):
            pltpu.make_async_copy(ref.at[rows], ref.at[rows], in_sem.at[n, k]).wait()

    run_ups = {(0, 0): (0, 24), (0, 1): (1, 48), (1, 1): (2, 64), (2, 1): (2, 80), (3, 0): (0, 8)}
    halo_slot = (3, 4)
    keeps = ((0, 1, 2), (0, 3))
    load(0)

    barrier = pltpu.get_barrier_semaphore()
    for other in others:
        for c in range(2):
            pl.semaphore_signal(barrier, inc=1, device_id=(2 * other + c, lat), device_id_type=MESH)
    pl.semaphore_signal(barrier, inc=1, device_id=(2 * chip + 1 - core, lat), device_id_type=MESH)
    inner_low, inner_high = lat > 0, lat < 3

    @pl.when(inner_low)
    def _():
        pl.semaphore_signal(barrier, inc=1, device_id=(me, lat - 1), device_id_type=MESH)

    @pl.when(inner_high)
    def _():
        pl.semaphore_signal(barrier, inc=1, device_id=(me, lat + 1), device_id_type=MESH)

    w_copies = [
        pltpu.make_async_copy(w_in, win, w_sem.at[0]),
        pltpu.make_async_copy(w_out, wout, w_sem.at[1]),
        pltpu.make_async_copy(mean_w, wi.at[pl.ds(K, HID - K)], w_sem.at[2]),
    ]
    lane = lax.broadcasted_iota(jnp.int32, (8, 128), 1)
    sub = lax.broadcasted_iota(jnp.int32, (8, 128), 0)
    odd = lax.rem(sub, 2) == 1
    wide_sub = lax.broadcasted_iota(jnp.int32, (8, LON), 0)
    wide_lane = lax.broadcasted_iota(jnp.int32, (8, LON), 1)

    def open_lon(b):
        here = msk[b]
        ox[b] = jnp.where(wide_lane < LON - 1, here * pltpu.roll(here, LON - 1, 1), 0.0)
        oxm[b] = jnp.where(wide_lane > 0, here * pltpu.roll(here, 1, 1), 0.0)

    def open_up(b):
        oy[b] = msk[b] * jnp.where(wide_sub == 7, pltpu.roll(msk[b + 1], 7, 0), pltpu.roll(msk[b], 7, 0))

    def open_down(b):
        oym[b] = msk[b] * jnp.where(wide_sub == 0, pltpu.roll(msk[b - 1], 1, 0), pltpu.roll(msk[b], 1, 0))

    def stacked(ref, b, j):
        part = [ref[b, j : j + 1, 128 * ct : 128 * ct + 128] for ct in range(4)]
        return jnp.where(sub < 4, jnp.where(sub < 2, part[0], part[1]), jnp.where(sub < 6, part[2], part[3]))

    def left_lon(b):
        for j in range(BLOCK):
            right, leftward = stacked(ox, b, j), stacked(oxm, b, j)
            oxl[0, b, j] = jnp.where(odd, leftward, right)
            oxl[1, b, j] = jnp.where(odd, right, leftward)
            ml[b, j] = stacked(msk, b, j)

    def left_up(b):
        for j in range(BLOCK):
            oyl[0, b, j] = stacked(oy, b, j)

    def left_down(b):
        for j in range(BLOCK):
            oyl[1, b, j] = stacked(oym, b, j)

    small[0].wait()
    msk[pl.ds(1, 12)] = mk[...].astype(F32).reshape(12, 8, LON)

    def inner_openings(b, _):
        open_lon(b)
        open_up(b)
        open_down(b)
        left_lon(b)
        left_up(b)
        left_down(b)
        return 0

    def first_openings(b, _):
        open_lon(b)
        open_up(b)
        left_lon(b)
        left_up(b)
        return 0

    def second_openings(b, _):
        open_down(b)
        left_down(b)
        return 0

    lax.fori_loop(4, 8, first_openings, 0)
    load(1)
    small[1].wait()
    steps = jnp.full((8, 128), counts[0], jnp.int32)
    rate = jnp.full((8, 128), speed[me], F32) / steps.astype(F32)

    def wide(v):
        return jnp.concatenate([v] * 4, axis=1)

    def propagate(n, side, substep):
        a = jnp.where(steps > substep, rate, 0.0)
        coef = [
            (wide(a * tb[0, pl.ds(16 * side + 8 * g, 8), :]), wide(a * tb[1, pl.ds(16 * side + 8 * g, 8), :]))
            for g in range(2)
        ]
        coef_l = (a * tb[0, pl.ds(32 + 8 * side, 8), :], a * tb[1, pl.ds(32 + 8 * side, 8), :])
        open_y = oym if side else oy

        def block(field, left, base, at, places, carry, source=None):
            field_in, left_in, base_in = source or (field, left, base)
            flows = list(carry)
            for j in places:
                i = base + j
                e = (at, j)
                row = (at, slice(j, j + 1), slice(None))
                oy_row = open_y[row]
                for g in range(2):
                    right = g == side
                    x = field_in[base_in + j, pl.ds(8 * g, 8), :]
                    if substep == 0:
                        x = x * msk[row]
                    o = x * coef[g][0] * (ox if right else oxm)[row]
                    p = x * coef[g][1] * oy_row
                    inflow = pltpu.roll(o, 1 if right else LON - 1, 1)
                    field[i, pl.ds(8 * g, 8), :] = x - o + inflow - p + flows[g]
                    flows[g] = p
                x = left_in[base_in + j]
                if substep == 0:
                    x = x * ml[e]
                o = x * coef_l[0] * oxl[(side, *e)]
                p = x * coef_l[1] * oyl[(side, *e)]
                up = pltpu.roll(o, 1, 1)
                up = jnp.where(lane == 0, pltpu.roll(up, 2, 0), up)
                down = pltpu.roll(o, 127, 1)
                down = jnp.where(lane == 127, pltpu.roll(down, 6, 0), down)
                inflow = jnp.where(odd, down, up) if side == 0 else jnp.where(odd, up, down)
                left[i] = x - o + inflow - p + flows[2]
                flows[2] = p
            return tuple(flows)

        low, high = PIECES[n] // BLOCK, (PIECES[n] + PIECE) // BLOCK
        edge = 5 - side
        if n == edge or (n, side) in run_ups:
            slot = halo_slot[side] if n == edge else run_ups[n, side][0]
            zero = jnp.zeros((8, LON), F32)
            start = (zero, zero, jnp.zeros((8, 128), F32))
            places = range(HALO - 1, -1, -1) if side else range(HALO, BLOCK)
            source = None
            if substep == 0 and n != edge:
                source = (fields[side], lefts[side], run_ups[n, side][1])
            start = block(run.at[slot], run_l.at[slot], 0, high + 1 if side else low, places, start, source)
        else:
            start = (flow[side, substep, 0:8], flow[side, substep, 8:16], flow_l[side, substep])

        def main(k, carry):
            b = high - 1 - k if side else low + k
            places = range(BLOCK - 1, -1, -1) if side else range(BLOCK)
            return block(fields[side], lefts[side], b * BLOCK, b + 1, places, carry)

        end = lax.fori_loop(0, high - low, main, start)
        if n in keeps[side]:
            flow[side, substep, 0:8] = end[0]
            flow[side, substep, 8:16] = end[1]
            flow_l[side, substep] = end[2]

    def passes(n, side):
        for substep in range(NSUB):
            propagate(n, side, substep)

    def mask_copy(up):
        return pltpu.make_async_remote_copy(
            mk.at[pl.ds(88, 8)] if up else mk.at[pl.ds(0, 8)],
            mh.at[0 if up else 1],
            mask_send.at[0 if up else 1],
            mask_recv.at[0 if up else 1],
            device_id=(me, lat + 1 if up else lat - 1),
            device_id_type=MESH,
        )

    def halo_copies(up):
        side = 0 if up else 1
        src, dst = (ROWS - HALO, HALO) if up else (0, 0)
        return [
            pltpu.make_async_remote_copy(
                ref.at[pl.ds(src, HALO)], to.at[halo_slot[side], pl.ds(dst, HALO)],
                halo_send.at[side, i], halo_recv.at[side, i],
                device_id=(me, lat + 1 if up else lat - 1), device_id_type=MESH,
            )
            for i, (ref, to) in enumerate(((fields[side], run), (lefts[side], run_l)))
        ]

    def edge_copies(up):
        return [mask_copy(up), *halo_copies(up)]

    def points(n, side):
        def row(j, _):
            r = PIECES[n] + j
            for ct in range(4):
                pb[r, pl.ds(PART * side + 16 * ct, 16), :] = fields[side][r, :, pl.ds(128 * ct, 128)].astype(BF16)
            if side == 1:
                pb[r, pl.ds(2 * PART, 16), :] = jnp.concatenate([lp[r], lm[r]], axis=0).astype(BF16)
            return 0

        lax.fori_loop(0, PIECE, row, 0)

    def send_copy(q, to, c, part):
        return pltpu.make_async_remote_copy(
            pb.at[q * GROUPS + 16 * c + to, part], rm.at[q, me, part], send_sem.at[q], recv_sem.at[q],
            device_id=(2 * to + c, lat), device_id_type=MESH,
        )

    def back_copy(q, to, c):
        return pltpu.make_async_remote_copy(
            ib.at[q, 2 * to + c], ri.at[q * GROUPS + 16 * core + chip], back_send.at[q], back_recv.at[q],
            device_id=(2 * to + c, lat), device_id_type=MESH,
        )

    def send(n, part=pl.ds(0, MSG)):
        q, c = PIECES[n] // GROUPS, PIECES[n] % GROUPS // PIECE

        for other in others:
            send_copy(q, other, c, part).start()

        @pl.when(core != c)
        def _():
            send_copy(q, chip, c, part).start()

        @pl.when(core == c)
        def _():
            pltpu.make_async_copy(
                pb.at[q * GROUPS + 16 * c + chip, part], rm.at[q, me, part], recv_sem.at[q]
            ).start()

    loaded(0)
    passes(0, 0)
    points(0, 0)
    neighbours = jnp.where(inner_low, 1, 0) + jnp.where(inner_high, 1, 0)
    pl.semaphore_wait(barrier, 2 * len(LATIN) + 1 + neighbours)
    send(0, pl.ds(0, PART))
    load(2)
    for copy in w_copies:
        copy.start()
    small[2].start()
    small[3].start()
    lax.fori_loop(5, 8, second_openings, 0)
    passes(0, 1)
    points(0, 1)
    send(0, pl.ds(PART, MSG - PART))
    loaded(1)
    loaded(2)

    @pl.when(inner_high)
    def _():
        for copy in edge_copies(True):
            copy.start()

    @pl.when(inner_low)
    def _():
        for copy in edge_copies(False):
            copy.start()

    lax.fori_loop(2, 5, inner_openings, 0)
    lax.fori_loop(8, 12, inner_openings, 0)
    def piece(n):
        for side in range(2):
            passes(n, side)
            points(n, side)
        send(n)

    for n in (1, 2, 3):
        piece(n)

    def select_columns(i, _):
        rows = pl.ds(pl.multiple_of(i * 384, 384), 384)
        wi[rows, :] = jnp.dot(win[rows, :], perm[...], preferred_element_type=F32).astype(BF16)
        return 0

    def select_rows(i, _):
        rows = pl.ds(pl.multiple_of(i * 384, 384), 384)
        wo[rows, pl.ds(0, K)] = jnp.dot(perm[rows, :], wout[...], preferred_element_type=F32).astype(BF16)
        return 0

    def build(across):
        def tile(i, _):
            start = pl.multiple_of(i * 128, 128)
            rows = start + lax.broadcasted_iota(jnp.int32, (128, K), 0)
            cols = lax.broadcasted_iota(jnp.int32, (128, K), 1)
            hit = natural(cols) == rows if across else natural(rows) == cols
            perm[pl.ds(start, 128), :] = jnp.where(hit, 1.0, 0.0).astype(BF16)
            return 0

        lax.fori_loop(0, K // 128, tile, 0)

    @pl.when(inner_low)
    def _():
        for copy in edge_copies(True):
            copy.wait_recv()

    @pl.when(inner_high)
    def _():
        for copy in edge_copies(False):
            copy.wait_recv()

    @pl.when(inner_high)
    def _():
        for copy in edge_copies(True):
            copy.wait_send()

    @pl.when(inner_low)
    def _():
        for copy in edge_copies(False):
            copy.wait_send()

    @pl.when(jnp.logical_not(inner_low))
    def _():
        mh[0] = jnp.zeros((8, LON), jnp.int32)
        run[halo_slot[0], pl.ds(HALO, HALO)] = jnp.zeros((HALO, 16, LON), F32)
        run_l[halo_slot[0], pl.ds(HALO, HALO)] = jnp.zeros((HALO, 8, 128), F32)

    @pl.when(jnp.logical_not(inner_high))
    def _():
        mh[1] = jnp.zeros((8, LON), jnp.int32)
        run[halo_slot[1], pl.ds(0, HALO)] = jnp.zeros((HALO, 16, LON), F32)
        run_l[halo_slot[1], pl.ds(0, HALO)] = jnp.zeros((HALO, 8, 128), F32)

    msk[0] = mh[0].astype(F32)
    msk[13] = mh[1].astype(F32)
    for b in (0, 1, 12, 13):
        open_lon(b)
        left_lon(b)
    for b in (0, 1, 12):
        open_up(b)
        left_up(b)
    for b in (1, 12, 13):
        open_down(b)
        left_down(b)

    for n in (4, 5):
        piece(n)

    for copy in w_copies:
        copy.wait()
    build(True)
    lax.fori_loop(0, 3, select_columns, 0)

    build(False)
    lax.fori_loop(0, 3, select_rows, 0)
    wo[:, pl.ds(K, HID - K)] = jnp.zeros((K, HID - K), BF16)

    small[2].wait()
    small[3].wait()

    def rates(i, _):
        start = pl.multiple_of(i * 128, 128)
        place = start + lax.broadcasted_iota(jnp.int32, (128, NFREQ), 0)
        freq, _ = component(place)
        pick = jnp.where(freq == lax.broadcasted_iota(jnp.int32, (128, NFREQ), 1), 0.5, 0.0)
        _, turn = component(start + lax.broadcasted_iota(jnp.int32, (128, NDIR), 0))
        hit = turn == lax.broadcasted_iota(jnp.int32, (128, NDIR), 1)
        for src, dst in ((gr, gain), (dp, damp)):
            rows = jnp.dot(pick, src[...], preferred_element_type=F32, precision=lax.Precision.HIGHEST)
            picked = jnp.sum(jnp.where(hit, rows, 0.0), axis=1, keepdims=True)
            dst[pl.ds(start, 128), :] = jnp.broadcast_to(picked, (128, 128))
        return 0

    lax.fori_loop(0, K // 128, rates, 0)

    def sources(q):
        lf[...] = rm[q, :, pl.ds(2 * PART, 16), :].reshape(16 * GROUPS, 128).astype(F32)
        for ct in range(4):
            for i in range(2):
                rl[pl.ds(64 * i, 64), pl.ds(128 * ct, 128)] = lf[pl.ds(2 * ct + i, 64, stride=8), :].astype(BF16)

        def both(q, which, ct):
            return jnp.concatenate(
                [rm[q, which, pl.ds(PART * side + 16 * ct, 16), :] for side in range(2)], axis=1
            )

        def right_side():
            main = [both(q, slice(None), ct).reshape(MAIN * GROUPS, 128) for ct in range(4)]
            return jnp.concatenate([jnp.concatenate(main, axis=1), rl[...]], axis=0)

        for part in range(2):
            hidden = jnp.dot(wi[pl.ds(TILE1 * part, TILE1), :], right_side(), preferred_element_type=F32)
            sq[pl.ds(TILE1 * part, TILE1), :] = (hidden * hidden).astype(BF16)
            if part == 1:
                energy = hidden[K - TILE1 : K - TILE1 + 1] + hidden[K - TILE1 + 1 : K - TILE1 + 2]
                hq[...] = jnp.broadcast_to(energy / (1.0 + energy), (8, LON))
        square = sq[...]

        def rows_of(i, _):
            base = pl.multiple_of(i * TILE2, TILE2)
            dests = TILE2 // MAIN
            transfer = jnp.dot(wo[pl.ds(base, TILE2), :], square, preferred_element_type=F32)
            for ct in range(4):
                which = pl.ds(i * dests, dests)
                energy = both(q, which, ct).astype(F32).reshape(TILE2, 128)
                rate = gain[pl.ds(base, TILE2), :] - damp[pl.ds(base, TILE2), :] * hq[0:1, 128 * ct : 128 * ct + 128]
                result = energy * rate + 0.125 * transfer[:, 128 * ct : 128 * ct + 128]
                result = result.astype(BF16).reshape(dests, MAIN, 128)
                for side in range(2):
                    ib[q, which, pl.ds(PART * side + 16 * ct, 16), :] = result[:, 16 * side : 16 * side + 16]
            return 0

        lax.fori_loop(0, MAIN * GROUPS // TILE2, rows_of, 0)
        transfer = jnp.dot(wo[pl.ds(1024, 128), :], square, preferred_element_type=F32)
        for ct in range(4):
            cols = slice(128 * ct, 128 * ct + 128)
            rate = gain[pl.ds(1024, 128), :] - damp[pl.ds(1024, 128), :] * hq[0:1, cols]
            result = rl[:, cols].astype(F32) * rate + 0.125 * transfer[:, cols]
            for i in range(2):
                tl[pl.ds(2 * ct + i, 64, stride=8), :] = result[64 * i : 64 * i + 64]
        ib[q, :, pl.ds(2 * PART, 16), :] = tl[...].astype(BF16).reshape(GROUPS, 16, 128)

    def chunk(q):
        pltpu.make_async_copy(rm.at[q], rm.at[q], recv_sem.at[q]).wait()
        sources(q)
        for c in range(2):
            for other in others:
                back_copy(q, other, c).start()
        back_copy(q, chip, 1 - core).start()
        pltpu.make_async_copy(ib.at[q, me], ri.at[q * GROUPS + 16 * core + chip], back_recv.at[q]).start()

    for q in PHASES:
        chunk(q)

    for q in PHASES:
        pltpu.make_async_copy(
            ri.at[pl.ds(q * GROUPS, GROUPS)], ri.at[pl.ds(q * GROUPS, GROUPS)], back_recv.at[q]
        ).wait()

        def rows(b, _):
            block_at = q * (GROUPS // BLOCK) + b + 1
            for j in range(BLOCK):
                r = q * GROUPS + b * BLOCK + j
                for ct in range(4):
                    cols = pl.ds(128 * ct, 128)
                    sea = msk[block_at, j : j + 1, cols]
                    fp[r, :, cols] += ri[r, pl.ds(16 * ct, 16), :].astype(F32) * sea
                    fm[r, :, cols] += ri[r, pl.ds(PART + 16 * ct, 16), :].astype(F32) * sea
                left = ri[r, pl.ds(2 * PART, 16), :].astype(F32)
                lp[r] += left[0:8] * ml[block_at, j]
                lm[r] += left[8:16] * ml[block_at, j]
            return 0

        lax.fori_loop(0, GROUPS // BLOCK, rows, 0)

    sent = pb.at[pl.ds(0, 2 * len(LATIN) + 1)]
    for q in range(CHUNKS):
        pltpu.make_async_copy(sent, sent, send_sem.at[q]).wait()
        pltpu.make_async_copy(sent, sent, back_send.at[q]).wait()


def store(fp, fm, lp, lm, out, sem):
    for quadrant in range(4):
        side, i = divmod(quadrant, 2)
        for t in range(8):
            pltpu.make_async_copy((fp, fm)[side].at[:, 8 * i + t, :], out.at[0, direction(quadrant, t)], sem.at[0]).start()
        for ct in range(4):
            pltpu.make_async_copy(
                (lp, lm)[side].at[:, 2 * ct + i, :], out.at[0, direction(quadrant, 8), :, pl.ds(128 * ct, 128)], sem.at[0]
            ).start()
    for ref in (fp, fm, lp, lm):
        pltpu.make_async_copy(ref, ref, sem.at[0]).wait()


def local(spectrum, sea_mask, point_index, band_counts, sub_counts, mix_in, mix_out, growth, damping):
    speed = (1.4 * np.power(np.float64(0.93), np.arange(NFREQ))).astype(np.float32)
    raw = np.power(np.float64(1.1), np.arange(NFREQ))
    weight = np.repeat(raw / (NDIR * raw.sum()), NDIR).astype(np.float32)
    weight = weight[natural(np.arange(K), np.where)]
    high = weight.astype(jnp.bfloat16)
    low = (weight - high.astype(np.float32)).astype(jnp.bfloat16)
    mean_w = np.zeros((HID - K, K), jnp.bfloat16)
    mean_w[0], mean_w[1] = high, low
    hbm, smem = pl.BlockSpec(memory_space=pl.ANY), pl.BlockSpec(memory_space=pltpu.SMEM)
    dma, VM = pltpu.SemaphoreType.DMA, pltpu.VMEM
    masks = [VM((14, 8, LON), F32)]
    fields = pl.pallas_call(
        kernel,
        name="wave_step",
        out_shape=[VM((ROWS, 16, LON), F32)] * 2 + [VM((ROWS, 8, 128), F32)] * 2,
        in_specs=[hbm, hbm, smem, smem, hbm, hbm, hbm, hbm, hbm, hbm],
        out_specs=[pl.BlockSpec(memory_space=VM)] * 4,
        scratch_shapes=[
            VM((5, BLOCK, 16, LON), F32), VM((5, BLOCK, 8, 128), F32),
            VM((ROWS, LON), jnp.int32), VM((2, 48, 128), F32), *masks, VM((2, 8, LON), jnp.int32), *masks * 4,
            VM((2, 14, 8, 8, 128), F32), VM((2, 14, 8, 8, 128), F32), VM((14, 8, 8, 128), F32),
            VM((2, NSUB, 16, LON), F32), VM((2, NSUB, 8, 128), F32),
            VM((ROWS, MSG, 128), BF16), VM((CHUNKS, GROUPS, MSG, 128), BF16),
            VM((CHUNKS, GROUPS, MSG, 128), BF16), VM((ROWS, MSG, 128), BF16),
            VM((K, K), BF16), VM((K, K), BF16), VM((K, K), BF16), VM((HID, K), BF16), VM((K, HID), BF16),
            VM((NFREQ, NDIR), F32), VM((NFREQ, NDIR), F32), VM((K, 128), F32), VM((K, 128), F32),
            VM((HID, LON), BF16), VM((8, LON), F32), VM((16 * GROUPS, 128), F32), VM((128, LON), BF16),
            VM((16 * GROUPS, 128), F32),
            dma((3, 4)), dma((4,)), dma((2, 2)), dma((2, 2)), dma((2,)), dma((2,)), dma((3,)),
            dma((CHUNKS,)), dma((CHUNKS,)), dma((CHUNKS,)), dma((CHUNKS,)),
        ],
        compiler_params=pltpu.CompilerParams(
            collective_id=0, has_side_effects=True, vmem_limit_bytes=VMEM - FIELD_BYTES
        ),
    )(spectrum, sea_mask, sub_counts, jnp.asarray(speed), jnp.asarray(angle_tables()), mix_in, mix_out,
      jnp.asarray(mean_w), growth, damping)
    return pl.pallas_call(
        store,
        name="wave_store",
        out_shape=jax.ShapeDtypeStruct(spectrum.shape, F32),
        in_specs=[pl.BlockSpec(memory_space=VM)] * 4,
        out_specs=hbm,
        scratch_shapes=[dma((1,))],
        compiler_params=pltpu.CompilerParams(vmem_limit_bytes=1024 * 1024),
    )(*[pltpu.with_memory_space_constraint(field, VM) for field in fields])


def solution(mesh):
    return jax.shard_map(
        local,
        mesh=mesh,
        in_specs=(
            P("comp", None, "lat", None),
            P("lat", None),
            P("lat", None),
            P("lat"),
            P("comp"),
            P(),
            P(),
            P(),
            P(),
        ),
        out_specs=P("comp", None, "lat", None),
        check_vma=False,
    )
```
